128 devices in a mesh: section: 4 (over z), dom: 32 (over y, x, core).
Axes of the slice: x: 4, y: 4, z: 4, core: 2. Of those that a mesh axis runs over, the one named last changes fastest.
Arguments:
- features: bfloat16 [8, 32768, 256], P(None, 'dom'), may hold values from -6 to 6
- tile_src: int32 [8, 256, 4], P(None, 'dom'), may hold values from 0 to 11
- tile_val: bfloat16 [8, 32768, 512], P(None, 'dom'), may hold values from -0.25 to 0.25
- boundary_rows: int32 [8, 64, 256], P(None, 'dom'), may hold values from 0 to 1023
- boundary_count: int32 [8, 64], P(None, 'dom'), may hold values from 64 to 256, as said below
- weights: bfloat16 [8, 256, 256], P('section'), may hold values from -0.375 to 0.375
- gains: bfloat16 [8, 256], P('section'), may hold values from 0.099609375 to 1.8984375
Outputs:
- output: bfloat16 [8, 32768, 256], P('section', 'dom')
The draws below stay inside these ranges and needn't reach their ends.
Inputs may be any that keep to these rules, and one draw needn't show every extreme that they name: `boundary_count`: each micro-batch graph has a buffer with all 256 slots live.
All inputs are finite; a program needn't handle non-finite values.
Results may differ from the reference program's by a relative error of at most 0.019.
Values may be sent and summed in bfloat16 or wider, within the bound.
No kernel may reach another device: no remote copies, remote signals or barrier semaphores. Data moves between devices by JAX's collectives and lax.ppermute only.
A program may use at most 128 MiB of HBM per device.

```python
import jax
import jax.numpy as jnp
from jax import lax

D = 256
TILE = 128
K = 4
ROWS_DEV = 1024
BND = 256
MB = 8
WINDOW_LAYERS = 8
NODES = 32768
SENDS = 64
N_DOM = 32


def draw_boundary_count(key, part):
    base = jax.random.randint(key, (MB, SENDS), BND // 4, BND + 1)
    spot = jax.random.randint(jax.random.fold_in(key, 7), (MB,), 0, SENDS)
    hit = jnp.arange(SENDS, dtype=jnp.int32)[None, :] == spot[:, None]
    return jnp.where(hit, BND, base).astype(jnp.int32)


def place_ends(values, own_key, smallest, largest):
    spot = [jax.random.randint(jax.random.fold_in(own_key, axis), (), 0, length) for axis, length in enumerate(values.shape)]
    longest = values.shape.index(max(values.shape))
    next_to = spot[:longest] + [(spot[longest] + 1) % values.shape[longest]] + spot[longest + 1:]
    return values.at[tuple(spot)].set(smallest).at[tuple(next_to)].set(largest)


def level_of(stream_key, shape, shards, smallest, largest):
    def one(axis_at, blocks):
        steps = jax.random.uniform(jax.random.fold_in(jax.random.fold_in(stream_key, 6), axis_at), (blocks,), jnp.float32, smallest / len(shards), largest / len(shards))
        return jnp.repeat(jnp.exp(steps), shape[axis_at] // blocks).reshape((-1,) + (1,) * (len(shape) - axis_at - 1))

    loudness = one(*shards[0])
    for cut in shards[1:]:
        loudness = loudness * one(*cut)
    return loudness


def noise(stream_key, dims, spread, reach, pieces=(), kind=jnp.bfloat16):
    drawn = spread * jax.random.normal(stream_key, dims, jnp.float32)
    if pieces:
        drawn = drawn * level_of(stream_key, dims, pieces, -0.22, 0.18)
    return jnp.clip(drawn, -reach, reach).astype(kind)


def setup_inputs(seed: int = 0) -> dict:
    keys = jax.random.split(jax.random.key(seed), 8)
    features = noise(keys[0], (MB, NODES, D), 1.0, 6.0, ((1, 32),))
    tile_src = place_ends(jax.random.randint(keys[1], (MB, NODES // TILE, K), 0, (ROWS_DEV + 2 * BND) // TILE), jax.random.fold_in(keys[1], 1), 0, ((ROWS_DEV + 2 * BND) // TILE) - 1).astype(jnp.int32)
    tile_val = noise(keys[2], (MB, NODES, K * TILE), (K * TILE) ** -0.5, 0.25, ((1, 32),))
    boundary_rows = place_ends(jax.random.randint(keys[3], (MB, SENDS, BND), 0, ROWS_DEV), jax.random.fold_in(keys[3], 1), 0, ROWS_DEV - 1).astype(jnp.int32)
    boundary_count = draw_boundary_count(jax.random.fold_in(keys[7], 71), 0)
    weights = noise(keys[5], (WINDOW_LAYERS, D, D), D ** -0.5, 0.375, ((0, 4),))
    gains = jnp.clip(1.0 + 0.18 * jax.random.normal(keys[6], (WINDOW_LAYERS, D), jnp.float32), 0.099609375, 1.8984375).astype(jnp.bfloat16)
    return {"features": features, "tile_src": tile_src, "tile_val": tile_val, "boundary_rows": boundary_rows, "boundary_count": boundary_count, "weights": weights, "gains": gains}


def apply_layer(hidden, weight, gain, tile_src, tile_val, boundary_rows, boundary_count):
    parts = hidden.shape[0]
    rows_dev = hidden.shape[1]
    width = hidden.shape[2]
    bnd = boundary_rows.shape[-1]
    hidden_f = hidden.astype(jnp.float32)
    scale = lax.rsqrt(lax.optimization_barrier(jnp.mean(hidden_f * hidden_f, axis=-1, keepdims=True)) + 1e-06)
    normed = jax.nn.relu(hidden_f * scale * gain.astype(jnp.float32)).astype(jnp.bfloat16)
    picks = boundary_rows.reshape(parts, 2 * bnd)
    send = jnp.take_along_axis(normed, picks[:, :, None], axis=1).reshape(parts, 2, bnd, width)
    live = jnp.arange(bnd, dtype=jnp.int32)[None, None, :] < boundary_count.reshape(parts, 2)[:, :, None]
    send = jnp.where(live[:, :, :, None], send, jnp.zeros_like(send))
    from_left = jnp.roll(send[:, 1], 1, axis=0)
    from_right = jnp.roll(send[:, 0], -1, axis=0)
    extended = jnp.concatenate([from_left, normed, from_right], axis=1)
    tiles = extended.reshape(parts, -1, TILE, width)
    selected_rows = jax.vmap(lambda block, index: block[index])(tiles, tile_src)
    tiled_rows = rows_dev // TILE
    edge_link = tile_val.reshape(parts, tiled_rows, TILE, K, TILE).astype(jnp.float32)
    summed_output = jnp.einsum('niakc,nikcd->niad', edge_link, selected_rows.astype(jnp.float32))
    neighbour_total = summed_output.reshape(parts * rows_dev, width).astype(jnp.bfloat16)
    update = jnp.dot(neighbour_total, weight, preferred_element_type=jnp.float32)
    return (hidden_f + update.reshape(parts, rows_dev, width)).astype(jnp.bfloat16)

def reference(features, tile_src, tile_val, boundary_rows, boundary_count, weights, gains):
    parts = N_DOM
    rows_dev = features.shape[1] // parts

    def one_graph(index):
        hidden = features[index].reshape(parts, rows_dev, -1)
        sources = tile_src[index].reshape(parts, rows_dev // TILE, K)
        values = tile_val[index].reshape(parts, rows_dev, -1)
        picks = boundary_rows[index].reshape(parts, 2, -1)
        counts = boundary_count[index].reshape(parts, 2)
        for layer_idx in range(weights.shape[0]):
            hidden = apply_layer(hidden, weights[layer_idx], gains[layer_idx], sources, values, picks, counts)
        return hidden.reshape(parts * rows_dev, -1)
    return lax.map(one_graph, jnp.arange(features.shape[0], dtype=jnp.int32))
```

```python
import functools

import jax
import jax.numpy as jnp
from jax import lax
from jax.experimental import pallas as pl
from jax.experimental.pallas import tpu as pltpu
from jax.sharding import PartitionSpec as P

TILE = 128
K = 4
EPS = 1e-06
BF = jnp.bfloat16
F32 = jnp.float32
VMEM = pl.BlockSpec(memory_space=pltpu.VMEM)
SMEM = pl.BlockSpec(memory_space=pltpu.SMEM)
HBM = pl.BlockSpec(memory_space=pltpu.HBM)


def call(body, outs, in_specs, name, scratch=(), limit=8, flops=0):
    return pl.pallas_call(
        body,
        out_shape=[jax.ShapeDtypeStruct(s, BF) for s in outs],
        in_specs=in_specs,
        out_specs=[VMEM] * len(outs),
        scratch_shapes=list(scratch),
        name=name,
        cost_estimate=pl.CostEstimate(flops=flops, bytes_accessed=1 << 20, transcendentals=0),
        compiler_params=pltpu.CompilerParams(vmem_limit_bytes=limit << 20),
    )


def normalise(hidden):
    mean = jnp.mean(hidden * hidden, axis=-1, keepdims=True)
    return jnp.maximum(hidden * lax.rsqrt(mean + EPS), 0.0).astype(BF)


def send_rows(chooser_ref, normed_ref, on_ref, off_ref):
    bnd = on_ref.shape[0]
    for at, out in ((bnd, off_ref), (0, on_ref)):
        out[...] = jnp.dot(
            chooser_ref[at : at + bnd, :], normed_ref[...], preferred_element_type=F32
        ).astype(BF)


def prologue_body(info_ref, count_ref, rows_ref, feat_ref, h_ref, nrm_ref, sel_ref, on_ref, off_ref, sem):
    graph, parity = info_ref[0], info_ref[1]
    copy = pltpu.make_async_copy(feat_ref.at[graph], h_ref, sem)
    copy.start()
    bnd = on_ref.shape[0]
    lane = lax.broadcasted_iota(jnp.int32, (1, bnd), 1)
    for at, buf in ((bnd, parity), (0, 1 - parity)):
        rows = rows_ref[graph, pl.ds(buf, 1), :]
        rows = jnp.where(lane < count_ref[buf, graph], rows, -1)
        column = jnp.broadcast_to(rows.astype(F32), (TILE, bnd)).T
        for c in range(sel_ref.shape[1] // TILE):
            ids = lax.broadcasted_iota(jnp.int32, (bnd, TILE), 1) + c * TILE
            hit = column == ids.astype(F32)
            sel_ref[at : at + bnd, c * TILE : (c + 1) * TILE] = jnp.where(hit, 1.0, 0.0).astype(BF)
    copy.wait()
    nrm_ref[...] = normalise(h_ref[...].astype(F32))
    send_rows(sel_ref, nrm_ref, on_ref, off_ref)


def fetch_body(info_ref, val_ref, tv_ref, sem):
    copy = pltpu.make_async_copy(val_ref.at[info_ref[0]], tv_ref, sem)
    copy.start()
    copy.wait()


def scale_body(w_ref, gain_ref, out_ref):
    width = w_ref.shape[1]
    gain = gain_ref[...].astype(F32)
    for k in range(w_ref.shape[0]):
        column = jnp.broadcast_to(gain[k : k + 1, :], (width, width)).T
        out_ref[k] = (w_ref[k].astype(F32) * column).astype(BF)


def order_body(count, info_ref, *refs):
    parts, out = refs[:count], refs[count]
    section = info_ref[2]
    per = parts[0].shape[0]
    for shift, part in enumerate(parts):
        source = lax.rem(section - shift + count, count)
        for k in range(per):
            out[source * per + k] = part[k]


def layer_body(layer, last, info_ref, src_ref, h_ref, nrm_ref, on_in, off_in, tv_ref, sel_ref, w_ref, *rest):
    if last:
        out_h, ext, agg = rest
    else:
        out_h, out_n, on_ref, off_ref, ext, agg = rest
    graph, parity = info_ref[0], info_ref[1]
    rows_dev = h_ref.shape[0]
    bnd = on_in.shape[0]
    own, half = rows_dev // TILE, bnd // TILE
    ext[0:own] = nrm_ref[...].reshape(own, TILE, -1)
    ext[own : own + half] = on_in[...].reshape(half, TILE, -1)
    ext[own + half : own + 2 * half] = off_in[...].reshape(half, TILE, -1)
    left = jnp.where(parity == 0, own + half, own)
    right = jnp.where(parity == 0, own, own + half)
    for i in range(own):
        picked = []
        for k in range(K):
            t = src_ref[graph, k, i]
            at = jnp.where(t < half, left + t, jnp.where(t < half + own, t - half, right + t - half - own))
            picked.append(ext[at])
        agg[i * TILE : (i + 1) * TILE, :] = jnp.dot(
            tv_ref[i * TILE : (i + 1) * TILE, :], jnp.concatenate(picked, axis=0), preferred_element_type=F32
        ).astype(BF)
    step = 256
    for r in range(0, rows_dev, step):
        rows = slice(r, r + step)
        update = jnp.dot(agg[rows, :], w_ref[layer], preferred_element_type=F32)
        new = (h_ref[rows, :].astype(F32) + update).astype(BF)
        out_h[rows, :] = new
        if not last:
            out_n[rows, :] = normalise(new.astype(F32))
    if not last:
        send_rows(sel_ref, out_n, on_ref, off_ref)


def on_device(features, tile_src, tile_val, boundary_rows, boundary_count, weights, gains):
    sections = lax.axis_size("section")
    doms = lax.axis_size("dom")
    section_id = lax.axis_index("section")
    dom_id = lax.axis_index("dom")
    graphs, rows_dev, width = features.shape
    bnd = boundary_rows.shape[-1]
    per_section = graphs // sections
    layers = weights.shape[0] * sections
    on_pairs = [(i, i ^ 1) for i in range(doms)]
    off_pairs = [(i, (i + (1 if i % 2 else -1)) % doms) for i in range(doms)]
    infos = [
        jnp.stack([section_id * per_section + g, dom_id % 2, section_id]).astype(jnp.int32)
        for g in range(per_section)
    ]

    def exchange(on, off):
        return lax.ppermute(on, "dom", on_pairs), lax.ppermute(off, "dom", off_pairs)

    tile_src = jnp.swapaxes(tile_src, 1, 2)
    boundary_count = jnp.swapaxes(boundary_count, 0, 1)
    features, tile_val = (pltpu.with_memory_space_constraint(x, pltpu.HBM) for x in (features, tile_val))
    state = []
    for info in infos:
        result = call(
            prologue_body,
            [(rows_dev, width), (rows_dev, width), (2 * bnd, rows_dev), (bnd, width), (bnd, width)],
            [SMEM, SMEM, VMEM, HBM],
            "prologue",
            [pltpu.SemaphoreType.DMA],
        )(info, boundary_count, boundary_rows, features)
        weights, *result = lax.optimization_barrier((weights, *result))
        h, nrm, sel, on, off = result
        state.append([h, nrm, sel, *exchange(on, off)])
    scaled = call(scale_body, [weights.shape], [VMEM, VMEM], "scale")(weights, gains)[0]
    parts = [scaled] + [
        lax.ppermute(scaled, "section", [(i, (i + shift) % sections) for i in range(sections)])
        for shift in range(1, sections)
    ]
    values = [
        call(fetch_body, [(rows_dev, K * TILE)], [SMEM, HBM], "fetch", [pltpu.SemaphoreType.DMA])(info, tile_val)[0]
        for info in infos
    ]
    w_all = call(
        functools.partial(order_body, sections), [(layers, width, width)], [SMEM] + [VMEM] * sections, "order"
    )(infos[0], *parts)[0]
    outputs = [None] * per_section
    for layer in range(layers):
        last = layer == layers - 1
        for g, info in enumerate(infos):
            h, nrm, sel, on, off = state[g]
            outs = [(rows_dev, width)]
            if not last:
                outs += [(rows_dev, width), (bnd, width), (bnd, width)]
            result = call(
                functools.partial(layer_body, layer, last),
                outs,
                [SMEM, SMEM] + [VMEM] * 7,
                "layer",
                [
                    pltpu.VMEM(((rows_dev + 2 * bnd) // TILE, TILE, width), BF),
                    pltpu.VMEM((rows_dev, width), BF),
                ],
                flops=700_000_000,
            )(info, tile_src, h, nrm, on, off, values[g], sel, w_all)
            if last:
                outputs[g] = result[0]
            else:
                h, nrm, on, off = result
                state[g] = [h, nrm, sel, *exchange(on, off)]
    return jnp.stack(outputs, axis=0)


def solution(mesh):
    in_specs = (
        P(None, "dom", None),
        P(None, "dom", None),
        P(None, "dom", None),
        P(None, "dom", None),
        P(None, "dom"),
        P("section", None, None),
        P("section", None),
    )
    return jax.shard_map(
        on_device, mesh=mesh, in_specs=in_specs, out_specs=P("section", "dom", None), check_vma=False
    )
```

```python
import functools

import jax
import jax.numpy as jnp
from jax import lax
from jax.experimental import pallas as pl
from jax.experimental.pallas import tpu as pltpu
from jax.sharding import PartitionSpec as P

TILE = 128
K = 4
EPS = 1e-06
BF = jnp.bfloat16
F32 = jnp.float32
VMEM = pl.BlockSpec(memory_space=pltpu.VMEM)
HBM = pl.BlockSpec(memory_space=pltpu.HBM)


def call(body, outs, in_specs, name, scratch=(), limit=8, flops=0, ints=(), hbm_out=False):
    return pl.pallas_call(
        body,
        out_shape=[jax.ShapeDtypeStruct(s, BF) for s in outs] + [jax.ShapeDtypeStruct(s, jnp.int32) for s in ints],
        in_specs=in_specs,
        out_specs=[HBM if hbm_out else VMEM] * (len(outs) + len(ints)),
        scratch_shapes=list(scratch),
        name=name,
        cost_estimate=pl.CostEstimate(flops=flops, bytes_accessed=1 << 10, transcendentals=0),
        compiler_params=pltpu.CompilerParams(vmem_limit_bytes=limit << 20),
    )


def normalise(hidden):
    mean = jnp.mean(hidden * hidden, axis=-1, keepdims=True)
    return jnp.maximum(hidden * lax.rsqrt(mean + EPS), 0.0).astype(BF)


def send_rows(chooser_ref, normed_ref, on_ref, off_ref):
    bnd = on_ref.shape[0]
    for at, out in ((bnd, off_ref), (0, on_ref)):
        out[...] = jnp.dot(
            chooser_ref[at : at + bnd, :], normed_ref[...], preferred_element_type=F32
        ).astype(BF)


def dom_parity():
    return lax.rem(lax.axis_index("dom"), 2)


def graph_of(local, per_section):
    return lax.axis_index("section") * per_section + local


def chunked(source, target, sems):
    count = sems.shape[0]
    step = target.shape[0] // count
    copies = []
    for c in range(count):
        rows = pl.ds(c * step, step)
        copies.append(pltpu.make_async_copy(source.at[rows], target.at[rows], sems.at[c]))
    for copy in copies:
        copy.start()
    return copies


def prologue_body(local, per_section, early, *refs):
    feat, rows_hbm, count_hbm, src_hbm = refs[:4]
    refs = refs[4 + early :]
    h_ref, nrm_ref, sel_ref, on_ref, off_ref, idx_ref = refs[:6]
    rows_ref, count_ref, src_ref, sems, feat_sems = refs[6:]
    graph, parity = graph_of(local, per_section), dom_parity()
    small = [
        pltpu.make_async_copy(rows_hbm.at[graph], rows_ref, sems.at[0]),
        pltpu.make_async_copy(count_hbm, count_ref, sems.at[1]),
        pltpu.make_async_copy(src_hbm.at[graph], src_ref, sems.at[2]),
    ]
    for copy in small:
        copy.start()
    copies = chunked(feat.at[graph], h_ref, feat_sems)
    for copy in small:
        copy.wait()
    rows_dev = h_ref.shape[0]
    bnd = on_ref.shape[0]
    own, half = rows_dev // TILE, bnd // TILE
    counts = count_ref[...]
    here = lax.broadcasted_iota(jnp.int32, counts.shape, 1) == graph
    live = jnp.sum(jnp.where(here, counts, 0), axis=1, keepdims=True)
    lane = lax.broadcasted_iota(jnp.int32, rows_ref.shape, 1)
    rows = jnp.where(lane < live, rows_ref[...], -1).astype(F32)
    first = jnp.broadcast_to(rows[0:1, :], (TILE, bnd))
    second = jnp.broadcast_to(rows[1:2, :], (TILE, bnd))
    even = parity == 0
    for at, picked in ((0, jnp.where(even, second, first)), (bnd, jnp.where(even, first, second))):
        column = picked.T
        for c in range(rows_dev // TILE):
            ids = lax.broadcasted_iota(jnp.int32, (bnd, TILE), 1) + c * TILE
            hit = column == ids.astype(F32)
            sel_ref[at : at + bnd, c * TILE : (c + 1) * TILE] = jnp.where(hit, 1.0, 0.0).astype(BF)
    t = src_ref[...]
    left = jnp.where(even, own + half, own)
    right = jnp.where(even, own, own + half)
    table = jnp.where(t < half, left + t, jnp.where(t < half + own, t - half, right + t - half - own))
    for i in range(own):
        for k in range(K):
            idx_ref[i * K + k : i * K + k + 1, :] = jnp.broadcast_to(table[k : k + 1, i : i + 1], (1, TILE))
    for c, copy in enumerate(copies):
        copy.wait()
        block = slice(c * rows_dev // len(copies), (c + 1) * rows_dev // len(copies))
        nrm_ref[block, :] = normalise(h_ref[block, :].astype(F32))
    send_rows(sel_ref, nrm_ref, on_ref, off_ref)


def fetch_body(per_section, val_ref, after_ref, *refs):
    outs, sems = refs[:per_section], refs[per_section]
    copies = []
    for g, out in enumerate(outs):
        copies += chunked(val_ref.at[graph_of(g, per_section)], out, sems.at[g])
    for copy in copies:
        copy.wait()


def scale_body(w_ref, gain_ref, after_ref, out_ref):
    width = w_ref.shape[1]
    gain = gain_ref[...].astype(F32)
    for k in range(w_ref.shape[0]):
        column = jnp.broadcast_to(gain[k : k + 1, :], (width, width)).T
        out_ref[k] = (w_ref[k].astype(F32) * column).astype(BF)


def order_body(count, *refs):
    parts, out = refs[:count], refs[count]
    section = lax.axis_index("section")
    per = parts[0].shape[0]
    for shift, part in enumerate(parts):
        source = lax.rem(section - shift + count, count)
        for k in range(per):
            out[source * per + k] = part[k]


def layer_body(layer, last, others, idx_ref, h_ref, nrm_ref, on_in, off_in, tv_ref, sel_ref, w_ref, *rest):
    done, rest = rest[:others], rest[others:]
    if last and others:
        out_ref, ext, agg, out_h, sems = rest
        copies = [pltpu.make_async_copy(done[g], out_ref.at[g], sems.at[g]) for g in range(others)]
        for copy in copies:
            copy.start()
    elif last:
        out_h, ext, agg = rest
    else:
        out_h, out_n, on_ref, off_ref, ext, agg = rest
    rows_dev = h_ref.shape[0]
    bnd = on_in.shape[0]
    own, half = rows_dev // TILE, bnd // TILE
    index = [idx_ref[j, 0] for j in range(own * K)]
    ext[0:own] = nrm_ref[...].reshape(own, TILE, -1)
    ext[own : own + half] = on_in[...].reshape(half, TILE, -1)
    ext[own + half : own + 2 * half] = off_in[...].reshape(half, TILE, -1)
    for i in range(own):
        picked = [ext[index[i * K + k]] for k in range(K)]
        agg[i * TILE : (i + 1) * TILE, :] = jnp.dot(
            tv_ref[i * TILE : (i + 1) * TILE, :], jnp.concatenate(picked, axis=0), preferred_element_type=F32
        ).astype(BF)
    step = 256
    for r in range(0, rows_dev, step):
        rows = slice(r, r + step)
        update = jnp.dot(agg[rows, :], w_ref[layer], preferred_element_type=F32)
        new = (h_ref[rows, :].astype(F32) + update).astype(BF)
        out_h[rows, :] = new
        if not last:
            out_n[rows, :] = normalise(new.astype(F32))
    if not last:
        send_rows(sel_ref, out_n, on_ref, off_ref)
    elif others:
        copies.append(pltpu.make_async_copy(out_h, out_ref.at[others], sems.at[others]))
        copies[-1].start()
        for copy in copies:
            copy.wait()


def on_device(features, tile_src, tile_val, boundary_rows, boundary_count, weights, gains):
    sections = lax.axis_size("section")
    doms = lax.axis_size("dom")
    graphs, rows_dev, width = features.shape
    bnd = boundary_rows.shape[-1]
    per_section = graphs // sections
    layers = weights.shape[0] * sections
    tiles = rows_dev // TILE
    on_pairs = [(i, i ^ 1) for i in range(doms)]
    off_pairs = [(i, (i + (1 if i % 2 else -1)) % doms) for i in range(doms)]

    def exchange(on, off):
        return lax.ppermute(on, "dom", on_pairs), lax.ppermute(off, "dom", off_pairs)

    tile_src = jnp.swapaxes(tile_src, 1, 2)
    boundary_count = jnp.swapaxes(boundary_count, 0, 1)
    features, tile_val, boundary_rows, boundary_count, tile_src = (
        pltpu.with_memory_space_constraint(x, pltpu.HBM)
        for x in (features, tile_val, boundary_rows, boundary_count, tile_src)
    )
    state = []
    early = ()
    for g in range(per_section):
        h, nrm, sel, on, off, idx = call(
            functools.partial(prologue_body, g, per_section, len(early)),
            [(rows_dev, width), (rows_dev, width), (2 * bnd, rows_dev), (bnd, width), (bnd, width)],
            [HBM] * 4 + [VMEM] * len(early),
            "prologue",
            [
                pltpu.VMEM((2, bnd), jnp.int32),
                pltpu.VMEM((2, graphs), jnp.int32),
                pltpu.VMEM((K, tiles), jnp.int32),
                pltpu.SemaphoreType.DMA((3,)),
                pltpu.SemaphoreType.DMA((4,)),
            ],
            ints=[(tiles * K, TILE)],
        )(features, boundary_rows, boundary_count, tile_src, *early)
        on, off = exchange(on, off)
        state.append([h, nrm, on, off, sel, idx])
        early = (state[0][2],)
    scaled = call(scale_body, [weights.shape], [VMEM] * 3, "scale")(weights, gains, *early)[0]
    parts = [scaled] + [
        lax.ppermute(scaled, "section", [(i, (i + shift) % sections) for i in range(sections)])
        for shift in range(1, sections)
    ]
    values = call(
        functools.partial(fetch_body, per_section),
        [(rows_dev, K * TILE)] * per_section,
        [HBM, VMEM],
        "fetch",
        [pltpu.SemaphoreType.DMA((per_section, 4))],
    )(tile_val, *early)
    w_all = call(functools.partial(order_body, sections), [(layers, width, width)], [VMEM] * sections, "order")(
        *parts
    )[0]
    outputs = []
    for layer in range(layers):
        last = layer == layers - 1
        for g in range(per_section):
            h, nrm, on, off, sel, idx = state[g]
            scratch = [pltpu.VMEM((tiles + 2 * bnd // TILE, TILE, width), BF), pltpu.VMEM((rows_dev, width), BF)]
            final = last and g == per_section - 1
            others = len(outputs) if final else 0
            if final:
                outs = [(per_section, rows_dev, width)]
                scratch += [pltpu.VMEM((rows_dev, width), BF), pltpu.SemaphoreType.DMA((per_section,))]
            elif last:
                outs = [(rows_dev, width)]
            else:
                outs = [(rows_dev, width), (rows_dev, width), (bnd, width), (bnd, width)]
            result = call(
                functools.partial(layer_body, layer, last, others),
                outs,
                [VMEM] * (8 + others),
                "layer",
                scratch,
                flops=1_000_000,
                hbm_out=final,
            )(idx, h, nrm, on, off, values[g], sel, w_all, *outputs[:others])
            if last:
                outputs.append(result[0])
            else:
                h, nrm, on, off = result
                state[g] = [h, nrm, *exchange(on, off), sel, idx]
    return outputs[-1]


def solution(mesh):
    in_specs = (
        P(None, "dom", None),
        P(None, "dom", None),
        P(None, "dom", None),
        P(None, "dom", None),
        P(None, "dom"),
        P("section", None, None),
        P("section", None),
    )
    return jax.shard_map(
        on_device, mesh=mesh, in_specs=in_specs, out_specs=P("section", "dom", None), check_vma=False
    )
```

```python
import functools

import jax
import jax.numpy as jnp
from jax import lax
from jax.experimental import pallas as pl
from jax.experimental.pallas import tpu as pltpu
from jax.sharding import PartitionSpec as P

TILE = 128
K = 4
EPS = 1e-06
BF = jnp.bfloat16
F32 = jnp.float32
VMEM = pl.BlockSpec(memory_space=pltpu.VMEM)
HBM = pl.BlockSpec(memory_space=pltpu.HBM)


def call(body, outs, in_specs, name, scratch=(), limit=8, flops=0, ints=(), hbm_out=False):
    return pl.pallas_call(
        body,
        out_shape=[jax.ShapeDtypeStruct(s, BF) for s in outs] + [jax.ShapeDtypeStruct(s, jnp.int32) for s in ints],
        in_specs=in_specs,
        out_specs=[HBM if hbm_out else VMEM] * (len(outs) + len(ints)),
        scratch_shapes=list(scratch),
        name=name,
        cost_estimate=pl.CostEstimate(flops=flops, bytes_accessed=1 << 10, transcendentals=0),
        compiler_params=pltpu.CompilerParams(vmem_limit_bytes=limit << 20),
    )


def normalise(hidden):
    mean = jnp.mean(hidden * hidden, axis=-1, keepdims=True)
    return jnp.maximum(hidden * lax.rsqrt(mean + EPS), 0.0).astype(BF)


def send_rows(chooser_ref, normed_ref, on_ref, off_ref):
    bnd = on_ref.shape[0]
    for at, out in ((bnd, off_ref), (0, on_ref)):
        out[...] = jnp.dot(
            chooser_ref[at : at + bnd, :], normed_ref[...], preferred_element_type=F32
        ).astype(BF)


def dom_parity():
    return lax.rem(lax.axis_index("dom"), 2)


def graph_of(local, per_section):
    return lax.axis_index("section") * per_section + local


def chunked(source, target, sems):
    count = sems.shape[0]
    step = target.shape[0] // count
    copies = []
    for c in range(count):
        rows = pl.ds(c * step, step)
        copies.append(pltpu.make_async_copy(source.at[rows], target.at[rows], sems.at[c]))
    for copy in copies:
        copy.start()
    return copies


def prologue_body(per_section, *refs):
    feat, rows_hbm, count_hbm, src_hbm, val_hbm, w_hbm, gain_hbm = refs[:7]
    graph_outs = [refs[7 + 6 * g : 13 + 6 * g] for g in range(per_section)]
    scaled_ref, *tables = refs[7 + 6 * per_section : 8 + 7 * per_section]
    rows_all, count_ref, src_all, w_ref, gain_ref, sems, small_sems, feat_sems, val_sems = refs[8 + 7 * per_section :]
    even = dom_parity() == 0
    graphs = [graph_of(g, per_section) for g in range(per_section)]
    count_copy = pltpu.make_async_copy(count_hbm, count_ref, sems.at[0])
    count_copy.start()
    small = [
        [
            pltpu.make_async_copy(rows_hbm.at[graph], rows_all.at[g], small_sems.at[g, 0]),
            pltpu.make_async_copy(src_hbm.at[graph], src_all.at[g], small_sems.at[g, 1]),
        ]
        for g, graph in enumerate(graphs)
    ]
    for pair in small:
        for copy in pair:
            copy.start()
    feat_copies = [
        chunked(feat.at[graph], graph_outs[g][0], feat_sems.at[g]) for g, graph in enumerate(graphs)
    ]
    later = [
        pltpu.make_async_copy(gain_hbm, gain_ref, sems.at[1]),
        pltpu.make_async_copy(w_hbm, w_ref, sems.at[2]),
    ]
    for copy in later:
        copy.start()
    val_copies = []
    for g, graph in enumerate(graphs):
        val_copies += chunked(val_hbm.at[graph], graph_outs[g][5], val_sems.at[g])
    count_copy.wait()
    for g, graph in enumerate(graphs):
        h_ref, nrm_ref, sel_ref, on_ref, off_ref, _ = graph_outs[g]
        rows_dev = h_ref.shape[0]
        bnd = on_ref.shape[0]
        own, half = rows_dev // TILE, bnd // TILE
        for copy in small[g]:
            copy.wait()
        counts = count_ref[...]
        here = lax.broadcasted_iota(jnp.int32, counts.shape, 1) == graph
        live = jnp.sum(jnp.where(here, counts, 0), axis=1, keepdims=True)
        raw = rows_all[g]
        lane = lax.broadcasted_iota(jnp.int32, raw.shape, 1)
        rows = jnp.where(lane < live, raw, -1).astype(F32)
        first = jnp.broadcast_to(rows[0:1, :], (TILE, bnd))
        second = jnp.broadcast_to(rows[1:2, :], (TILE, bnd))
        for at, picked in ((0, jnp.where(even, second, first)), (bnd, jnp.where(even, first, second))):
            column = picked.T
            for c in range(rows_dev // TILE):
                ids = lax.broadcasted_iota(jnp.int32, (bnd, TILE), 1) + c * TILE
                hit = column == ids.astype(F32)
                sel_ref[at : at + bnd, c * TILE : (c + 1) * TILE] = jnp.where(hit, 1.0, 0.0).astype(BF)
        t = src_all[g]
        left = jnp.where(even, own + half, own)
        right = jnp.where(even, own, own + half)
        table = jnp.where(t < half, left + t, jnp.where(t < half + own, t - half, right + t - half - own))
        for i in range(own):
            for k in range(K):
                tables[g][i * K + k : i * K + k + 1, :] = jnp.broadcast_to(table[k : k + 1, i : i + 1], (1, TILE))
        for c, copy in enumerate(feat_copies[g]):
            copy.wait()
            step = rows_dev // len(feat_copies[g])
            block = slice(c * step, (c + 1) * step)
            nrm_ref[block, :] = normalise(h_ref[block, :].astype(F32))
        send_rows(sel_ref, nrm_ref, on_ref, off_ref)
    for copy in later:
        copy.wait()
    scale(w_ref, gain_ref, scaled_ref)
    for copy in val_copies:
        copy.wait()


def scale(w_ref, gain_ref, out_ref):
    width = w_ref.shape[1]
    gain = gain_ref[...].astype(F32)
    for k in range(w_ref.shape[0]):
        column = jnp.broadcast_to(gain[k : k + 1, :], (width, width)).T
        out_ref[k] = (w_ref[k].astype(F32) * column).astype(BF)


def gate_body(after_ref, out_ref):
    out_ref[...] = after_ref[: out_ref.shape[0], : out_ref.shape[1]]


def order_body(count, *refs):
    parts, out = refs[:count], refs[-1]
    section = lax.axis_index("section")
    per = parts[0].shape[0]
    for shift, part in enumerate(parts):
        source = lax.rem(section - shift + count, count)
        for k in range(per):
            out[source * per + k] = part[k]


def layer_body(layer, last, others, idx_ref, h_ref, nrm_ref, on_in, off_in, tv_ref, sel_ref, w_ref, *rest):
    done, rest = rest[:others], rest[others:]
    if last and others:
        out_ref, ext, agg, out_h, sems = rest
        copies = [pltpu.make_async_copy(done[g], out_ref.at[g], sems.at[g]) for g in range(others)]
        for copy in copies:
            copy.start()
    elif last:
        out_h, ext, agg = rest
    else:
        out_h, out_n, on_ref, off_ref, ext, agg = rest
    rows_dev = h_ref.shape[0]
    bnd = on_in.shape[0]
    own, half = rows_dev // TILE, bnd // TILE
    index = [idx_ref[j, 0] for j in range(own * K)]
    ext[0:own] = nrm_ref[...].reshape(own, TILE, -1)
    ext[own : own + half] = on_in[...].reshape(half, TILE, -1)
    ext[own + half : own + 2 * half] = off_in[...].reshape(half, TILE, -1)
    for i in range(own):
        picked = [ext[index[i * K + k]] for k in range(K)]
        agg[i * TILE : (i + 1) * TILE, :] = jnp.dot(
            tv_ref[i * TILE : (i + 1) * TILE, :], jnp.concatenate(picked, axis=0), preferred_element_type=F32
        ).astype(BF)
    step = 256
    for r in range(0, rows_dev, step):
        rows = slice(r, r + step)
        update = jnp.dot(agg[rows, :], w_ref[layer], preferred_element_type=F32)
        new = (h_ref[rows, :].astype(F32) + update).astype(BF)
        out_h[rows, :] = new
        if not last:
            out_n[rows, :] = normalise(new.astype(F32))
    if not last:
        send_rows(sel_ref, out_n, on_ref, off_ref)
    elif others:
        copies.append(pltpu.make_async_copy(out_h, out_ref.at[others], sems.at[others]))
        copies[-1].start()
        for copy in copies:
            copy.wait()


def on_device(features, tile_src, tile_val, boundary_rows, boundary_count, weights, gains):
    sections = lax.axis_size("section")
    doms = lax.axis_size("dom")
    graphs, rows_dev, width = features.shape
    bnd = boundary_rows.shape[-1]
    per_section = graphs // sections
    layers = weights.shape[0] * sections
    tiles = rows_dev // TILE
    on_pairs = [(i, i ^ 1) for i in range(doms)]
    off_pairs = [(i, (i + (1 if i % 2 else -1)) % doms) for i in range(doms)]

    def exchange(on, off):
        return lax.ppermute(on, "dom", on_pairs), lax.ppermute(off, "dom", off_pairs)

    tile_src = jnp.swapaxes(tile_src, 1, 2)
    boundary_count = jnp.swapaxes(boundary_count, 0, 1)
    features, tile_val, boundary_rows, boundary_count, tile_src, weights, gains = (
        pltpu.with_memory_space_constraint(x, pltpu.HBM)
        for x in (features, tile_val, boundary_rows, boundary_count, tile_src, weights, gains)
    )
    per_graph = [(rows_dev, width), (rows_dev, width), (2 * bnd, rows_dev), (bnd, width), (bnd, width)]
    per_graph += [(rows_dev, K * TILE)]
    results = call(
        functools.partial(prologue_body, per_section),
        per_graph * per_section + [weights.shape],
        [HBM] * 7,
        "prologue",
        [
            pltpu.VMEM((per_section, 2, bnd), jnp.int32),
            pltpu.VMEM((2, graphs), jnp.int32),
            pltpu.VMEM((per_section, K, tiles), jnp.int32),
            pltpu.VMEM(weights.shape, BF),
            pltpu.VMEM(gains.shape, BF),
            pltpu.SemaphoreType.DMA((3,)),
            pltpu.SemaphoreType.DMA((per_section, 2)),
            pltpu.SemaphoreType.DMA((per_section, 4)),
            pltpu.SemaphoreType.DMA((per_section, 4)),
        ],
        limit=16,
        ints=[(tiles * K, TILE)] * per_section,
    )(features, boundary_rows, boundary_count, tile_src, tile_val, weights, gains)
    scaled, *tables = results[6 * per_section :]
    state, values = [], []
    for g in range(per_section):
        h, nrm, sel, on, off, value = results[6 * g : 6 * g + 6]
        values.append(value)
        on = lax.ppermute(on, "dom", on_pairs)
        off, on = lax.optimization_barrier((off, on))
        off = lax.ppermute(off, "dom", off_pairs)
        state.append([h, nrm, on, off, sel, tables[g]])
    parts = [scaled] + [
        lax.ppermute(scaled, "section", [(i, (i + shift) % sections) for i in range(sections)])
        for shift in range(1, sections)
    ]
    gate = call(gate_body, [(16, TILE)], [VMEM], "gate")(state[0][3])[0]
    w_all = call(
        functools.partial(order_body, sections), [(layers, width, width)], [VMEM] * (sections + 1), "order"
    )(*parts, gate)[0]
    outputs = []
    for layer in range(layers):
        last = layer == layers - 1
        for g in range(per_section):
            h, nrm, on, off, sel, idx = state[g]
            scratch = [pltpu.VMEM((tiles + 2 * bnd // TILE, TILE, width), BF), pltpu.VMEM((rows_dev, width), BF)]
            final = last and g == per_section - 1
            others = len(outputs) if final else 0
            if final:
                outs = [(per_section, rows_dev, width)]
                scratch += [pltpu.VMEM((rows_dev, width), BF), pltpu.SemaphoreType.DMA((per_section,))]
            elif last:
                outs = [(rows_dev, width)]
            else:
                outs = [(rows_dev, width), (rows_dev, width), (bnd, width), (bnd, width)]
            result = call(
                functools.partial(layer_body, layer, last, others),
                outs,
                [VMEM] * (8 + others),
                "layer",
                scratch,
                flops=1_000_000,
                hbm_out=final,
            )(idx, h, nrm, on, off, values[g], sel, w_all, *outputs[:others])
            if last:
                outputs.append(result[0])
            else:
                h, nrm, on, off = result
                state[g] = [h, nrm, *exchange(on, off), sel, idx]
    return outputs[-1]


def solution(mesh):
    in_specs = (
        P(None, "dom", None),
        P(None, "dom", None),
        P(None, "dom", None),
        P(None, "dom", None),
        P(None, "dom"),
        P("section", None, None),
        P("section", None),
    )
    return jax.shard_map(
        on_device, mesh=mesh, in_specs=in_specs, out_specs=P("section", "dom", None), check_vma=False
    )
```

```python
import functools

import jax
import jax.numpy as jnp
from jax import lax
from jax.experimental import pallas as pl
from jax.experimental.pallas import tpu as pltpu
from jax.sharding import PartitionSpec as P

TILE = 128
K = 4
EPS = 1e-06
BF = jnp.bfloat16
F32 = jnp.float32
VMEM = pl.BlockSpec(memory_space=pltpu.VMEM)
HBM = pl.BlockSpec(memory_space=pltpu.HBM)


def call(body, outs, in_specs, name, scratch=(), limit=8, flops=0, ints=(), hbm_out=False):
    return pl.pallas_call(
        body,
        out_shape=[jax.ShapeDtypeStruct(s, BF) for s in outs] + [jax.ShapeDtypeStruct(s, jnp.int32) for s in ints],
        in_specs=in_specs,
        out_specs=[HBM if hbm_out else VMEM] * (len(outs) + len(ints)),
        scratch_shapes=list(scratch),
        name=name,
        cost_estimate=pl.CostEstimate(flops=flops, bytes_accessed=1 << 10, transcendentals=0),
        compiler_params=pltpu.CompilerParams(vmem_limit_bytes=limit << 20),
    )


def normalise(hidden):
    mean = jnp.mean(hidden * hidden, axis=-1, keepdims=True)
    return jnp.maximum(hidden * lax.rsqrt(mean + EPS), 0.0).astype(BF)


def send_rows(chooser_ref, normed_ref, on_ref, off_ref):
    bnd = on_ref.shape[0]
    for at, out in ((bnd, off_ref), (0, on_ref)):
        out[...] = jnp.dot(
            chooser_ref[at : at + bnd, :], normed_ref[...], preferred_element_type=F32
        ).astype(BF)


def dom_parity():
    return lax.rem(lax.axis_index("dom"), 2)


def graph_of(local, per_section):
    return lax.axis_index("section") * per_section + local


def chunked(source, target, sems):
    count = sems.shape[0]
    step = target.shape[0] // count
    copies = []
    for c in range(count):
        rows = pl.ds(c * step, step)
        copies.append(pltpu.make_async_copy(source.at[rows], target.at[rows], sems.at[c]))
    for copy in copies:
        copy.start()
    return copies


def prologue_body(per_section, *refs):
    feat, rows_hbm, count_hbm, src_hbm, val_hbm, w_hbm, gain_hbm = refs[:7]
    graph_outs = [refs[7 + 6 * g : 13 + 6 * g] for g in range(per_section)]
    scaled_ref, mine_ref, *tables = refs[7 + 6 * per_section : 9 + 7 * per_section]
    rows_all, count_ref, src_all, w_ref, gain_ref, sems, small_sems, feat_sems, val_sems = refs[9 + 7 * per_section :]
    even = dom_parity() == 0
    graphs = [graph_of(g, per_section) for g in range(per_section)]
    count_copy = pltpu.make_async_copy(count_hbm, count_ref, sems.at[0])
    count_copy.start()
    small = [
        [
            pltpu.make_async_copy(rows_hbm.at[graph], rows_all.at[g], small_sems.at[g, 0]),
            pltpu.make_async_copy(src_hbm.at[graph], src_all.at[g], small_sems.at[g, 1]),
        ]
        for g, graph in enumerate(graphs)
    ]
    for pair in small:
        for copy in pair:
            copy.start()
    feat_copies = [
        chunked(feat.at[graph], graph_outs[g][0], feat_sems.at[g]) for g, graph in enumerate(graphs)
    ]
    later = [
        pltpu.make_async_copy(gain_hbm, gain_ref, sems.at[1]),
        pltpu.make_async_copy(w_hbm, w_ref, sems.at[2]),
    ]
    for copy in later:
        copy.start()
    val_copies = []
    for g, graph in enumerate(graphs):
        val_copies += chunked(val_hbm.at[graph], graph_outs[g][5], val_sems.at[g])
    count_copy.wait()
    for g, graph in enumerate(graphs):
        h_ref, nrm_ref, sel_ref, on_ref, off_ref, _ = graph_outs[g]
        rows_dev = h_ref.shape[0]
        bnd = on_ref.shape[0]
        own, half = rows_dev // TILE, bnd // TILE
        for copy in small[g]:
            copy.wait()
        counts = count_ref[...]
        here = lax.broadcasted_iota(jnp.int32, counts.shape, 1) == graph
        live = jnp.sum(jnp.where(here, counts, 0), axis=1, keepdims=True)
        raw = rows_all[g]
        lane = lax.broadcasted_iota(jnp.int32, raw.shape, 1)
        rows = jnp.where(lane < live, raw, -1).astype(F32)
        first = jnp.broadcast_to(rows[0:1, :], (TILE, bnd))
        second = jnp.broadcast_to(rows[1:2, :], (TILE, bnd))
        for at, picked in ((0, jnp.where(even, second, first)), (bnd, jnp.where(even, first, second))):
            column = picked.T
            for c in range(rows_dev // TILE):
                ids = lax.broadcasted_iota(jnp.int32, (bnd, TILE), 1) + c * TILE
                hit = column == ids.astype(F32)
                sel_ref[at : at + bnd, c * TILE : (c + 1) * TILE] = jnp.where(hit, 1.0, 0.0).astype(BF)
        t = src_all[g]
        left = jnp.where(even, own + half, own)
        right = jnp.where(even, own, own + half)
        table = jnp.where(t < half, left + t, jnp.where(t < half + own, t - half, right + t - half - own))
        for i in range(own):
            for k in range(K):
                tables[g][i * K + k : i * K + k + 1, :] = jnp.broadcast_to(table[k : k + 1, i : i + 1], (1, TILE))
        for c, copy in enumerate(feat_copies[g]):
            copy.wait()
            step = rows_dev // len(feat_copies[g])
            block = slice(c * step, (c + 1) * step)
            nrm_ref[block, :] = normalise(h_ref[block, :].astype(F32))
        send_rows(sel_ref, nrm_ref, on_ref, off_ref)
    for copy in later:
        copy.wait()
    scale(w_ref, gain_ref, scaled_ref)
    mine_ref[...] = scaled_ref[dom_parity()]
    for copy in val_copies:
        copy.wait()


def scale(w_ref, gain_ref, out_ref):
    width = w_ref.shape[1]
    gain = gain_ref[...].astype(F32)
    for k in range(w_ref.shape[0]):
        column = jnp.broadcast_to(gain[k : k + 1, :], (width, width)).T
        out_ref[k] = (w_ref[k].astype(F32) * column).astype(BF)


def pack_body(after_ref, *refs):
    for k, part in enumerate(refs[:-1]):
        refs[-1][k] = part[...]


def order_body(scaled_ref, mine_ref, swapped_ref, out_ref):
    section = lax.axis_index("section")
    parity = dom_parity()
    count = mine_ref.shape[0] + 1
    for k in range(2):
        out_ref[section * 2 + k] = scaled_ref[k]
    for shift in range(1, count):
        source = lax.rem(section - shift + count, count)
        out_ref[source * 2 + parity] = mine_ref[shift - 1]
        out_ref[source * 2 + 1 - parity] = swapped_ref[shift - 1]


def layer_body(layer, last, others, idx_ref, h_ref, nrm_ref, on_in, off_in, tv_ref, sel_ref, w_ref, *rest):
    done, rest = rest[:others], rest[others:]
    if last and others:
        out_ref, ext, agg, out_h, sems = rest
        copies = [pltpu.make_async_copy(done[g], out_ref.at[g], sems.at[g]) for g in range(others)]
        for copy in copies:
            copy.start()
    elif last:
        out_h, ext, agg = rest
    else:
        out_h, out_n, on_ref, off_ref, ext, agg = rest
    rows_dev = h_ref.shape[0]
    bnd = on_in.shape[0]
    own, half = rows_dev // TILE, bnd // TILE
    index = [idx_ref[j, 0] for j in range(own * K)]
    ext[0:own] = nrm_ref[...].reshape(own, TILE, -1)
    ext[own : own + half] = on_in[...].reshape(half, TILE, -1)
    ext[own + half : own + 2 * half] = off_in[...].reshape(half, TILE, -1)
    for i in range(own):
        picked = [ext[index[i * K + k]] for k in range(K)]
        agg[i * TILE : (i + 1) * TILE, :] = jnp.dot(
            tv_ref[i * TILE : (i + 1) * TILE, :], jnp.concatenate(picked, axis=0), preferred_element_type=F32
        ).astype(BF)
    step = 256
    for r in range(0, rows_dev, step):
        rows = slice(r, r + step)
        update = jnp.dot(agg[rows, :], w_ref[layer], preferred_element_type=F32)
        new = (h_ref[rows, :].astype(F32) + update).astype(BF)
        out_h[rows, :] = new
        if not last:
            out_n[rows, :] = normalise(new.astype(F32))
    if not last:
        send_rows(sel_ref, out_n, on_ref, off_ref)
    elif others:
        copies.append(pltpu.make_async_copy(out_h, out_ref.at[others], sems.at[others]))
        copies[-1].start()
        for copy in copies:
            copy.wait()


def on_device(features, tile_src, tile_val, boundary_rows, boundary_count, weights, gains):
    sections = lax.axis_size("section")
    doms = lax.axis_size("dom")
    graphs, rows_dev, width = features.shape
    bnd = boundary_rows.shape[-1]
    per_section = graphs // sections
    layers = weights.shape[0] * sections
    tiles = rows_dev // TILE
    on_pairs = [(i, i ^ 1) for i in range(doms)]
    off_pairs = [(i, (i + (1 if i % 2 else -1)) % doms) for i in range(doms)]

    def exchange(on, off):
        return lax.ppermute(on, "dom", on_pairs), lax.ppermute(off, "dom", off_pairs)

    tile_src = jnp.swapaxes(tile_src, 1, 2)
    boundary_count = jnp.swapaxes(boundary_count, 0, 1)
    features, tile_val, boundary_rows, boundary_count, tile_src, weights, gains = (
        pltpu.with_memory_space_constraint(x, pltpu.HBM)
        for x in (features, tile_val, boundary_rows, boundary_count, tile_src, weights, gains)
    )
    square = (width, width)
    per_graph = [(rows_dev, width), (rows_dev, width), (2 * bnd, rows_dev), (bnd, width), (bnd, width)]
    per_graph += [(rows_dev, K * TILE)]
    results = call(
        functools.partial(prologue_body, per_section),
        per_graph * per_section + [weights.shape, square],
        [HBM] * 7,
        "prologue",
        [
            pltpu.VMEM((per_section, 2, bnd), jnp.int32),
            pltpu.VMEM((2, graphs), jnp.int32),
            pltpu.VMEM((per_section, K, tiles), jnp.int32),
            pltpu.VMEM(weights.shape, BF),
            pltpu.VMEM(gains.shape, BF),
            pltpu.SemaphoreType.DMA((3,)),
            pltpu.SemaphoreType.DMA((per_section, 2)),
            pltpu.SemaphoreType.DMA((per_section, 4)),
            pltpu.SemaphoreType.DMA((per_section, 4)),
        ],
        limit=16,
        ints=[(tiles * K, TILE)] * per_section,
    )(features, boundary_rows, boundary_count, tile_src, tile_val, weights, gains)
    scaled, mine, *tables = results[6 * per_section :]
    state, values = [], []
    for g in range(per_section):
        h, nrm, sel, on, off, value = results[6 * g : 6 * g + 6]
        values.append(value)
        on = lax.ppermute(on, "dom", on_pairs)
        off, on = lax.optimization_barrier((off, on))
        off = lax.ppermute(off, "dom", off_pairs)
        state.append([h, nrm, on, off, sel, tables[g]])
    parts = [
        lax.ppermute(mine, "section", [(i, (i + shift) % sections) for i in range(sections)])
        for shift in range(1, sections)
    ]
    packed = call(pack_body, [(sections - 1, *square)], [VMEM] * sections, "pack")(state[0][3], *parts)[0]
    swapped = lax.ppermute(packed, "dom", on_pairs)
    w_all = call(order_body, [(layers, *square)], [VMEM] * 3, "order")(scaled, packed, swapped)[0]
    outputs = []
    for layer in range(layers):
        last = layer == layers - 1
        for g in range(per_section):
            h, nrm, on, off, sel, idx = state[g]
            scratch = [pltpu.VMEM((tiles + 2 * bnd // TILE, TILE, width), BF), pltpu.VMEM((rows_dev, width), BF)]
            final = last and g == per_section - 1
            others = len(outputs) if final else 0
            if final:
                outs = [(per_section, rows_dev, width)]
                scratch += [pltpu.VMEM((rows_dev, width), BF), pltpu.SemaphoreType.DMA((per_section,))]
            elif last:
                outs = [(rows_dev, width)]
            else:
                outs = [(rows_dev, width), (rows_dev, width), (bnd, width), (bnd, width)]
            result = call(
                functools.partial(layer_body, layer, last, others),
                outs,
                [VMEM] * (8 + others),
                "layer",
                scratch,
                flops=1_000_000,
                hbm_out=final,
            )(idx, h, nrm, on, off, values[g], sel, w_all, *outputs[:others])
            if last:
                outputs.append(result[0])
            else:
                h, nrm, on, off = result
                state[g] = [h, nrm, *exchange(on, off), sel, idx]
    return outputs[-1]


def solution(mesh):
    in_specs = (
        P(None, "dom", None),
        P(None, "dom", None),
        P(None, "dom", None),
        P(None, "dom", None),
        P(None, "dom"),
        P("section", None, None),
        P("section", None),
    )
    return jax.shard_map(
        on_device, mesh=mesh, in_specs=in_specs, out_specs=P("section", "dom", None), check_vma=False
    )
```

```python
import functools

import jax
import jax.numpy as jnp
from jax import lax
from jax.experimental import pallas as pl
from jax.experimental.pallas import tpu as pltpu
from jax.sharding import PartitionSpec as P

TILE = 128
K = 4
EPS = 1e-06
BF = jnp.bfloat16
F32 = jnp.float32
VMEM = pl.BlockSpec(memory_space=pltpu.VMEM)
HBM = pl.BlockSpec(memory_space=pltpu.HBM)


def call(body, outs, in_specs, name, scratch=(), limit=8, flops=0, ints=(), hbm_out=False):
    return pl.pallas_call(
        body,
        out_shape=[jax.ShapeDtypeStruct(s, BF) for s in outs] + [jax.ShapeDtypeStruct(s, jnp.int32) for s in ints],
        in_specs=in_specs,
        out_specs=[HBM if hbm_out else VMEM] * (len(outs) + len(ints)),
        scratch_shapes=list(scratch),
        name=name,
        cost_estimate=pl.CostEstimate(flops=flops, bytes_accessed=1 << 10, transcendentals=0),
        compiler_params=pltpu.CompilerParams(vmem_limit_bytes=limit << 20),
    )


def normalise(hidden):
    mean = jnp.mean(hidden * hidden, axis=-1, keepdims=True)
    return jnp.maximum(hidden * lax.rsqrt(mean + EPS), 0.0).astype(BF)


def send_rows(chooser_ref, normed_ref, on_ref, off_ref):
    bnd = on_ref.shape[0]
    for at, out in ((bnd, off_ref), (0, on_ref)):
        out[...] = jnp.dot(
            chooser_ref[at : at + bnd, :], normed_ref[...], preferred_element_type=F32
        ).astype(BF)


def dom_parity():
    return lax.rem(lax.axis_index("dom"), 2)


def graph_of(local, per_section):
    return lax.axis_index("section") * per_section + local


def chunked(source, target, sems):
    count = sems.shape[0]
    step = target.shape[0] // count
    copies = []
    for c in range(count):
        rows = pl.ds(c * step, step)
        copies.append(pltpu.make_async_copy(source.at[rows], target.at[rows], sems.at[c]))
    for copy in copies:
        copy.start()
    return copies


def prologue_body(per_section, *refs):
    feat, rows_hbm, count_hbm, src_hbm, w_hbm, gain_hbm = refs[:6]
    graph_outs = [refs[6 + 3 * g : 9 + 3 * g] for g in range(per_section)]
    on_all, off_all, scaled_ref, mine_ref, *tables = refs[6 + 3 * per_section : 10 + 4 * per_section]
    rows_all, count_ref, src_all, w_ref, gain_ref, sems, small_sems, feat_sems = refs[10 + 4 * per_section :]
    even = dom_parity() == 0
    graphs = [graph_of(g, per_section) for g in range(per_section)]
    count_copy = pltpu.make_async_copy(count_hbm, count_ref, sems.at[0])
    count_copy.start()
    small = [
        [
            pltpu.make_async_copy(rows_hbm.at[graph], rows_all.at[g], small_sems.at[g, 0]),
            pltpu.make_async_copy(src_hbm.at[graph], src_all.at[g], small_sems.at[g, 1]),
        ]
        for g, graph in enumerate(graphs)
    ]
    for pair in small:
        for copy in pair:
            copy.start()
    feat_copies = [
        chunked(feat.at[graph], graph_outs[g][0], feat_sems.at[g]) for g, graph in enumerate(graphs)
    ]
    later = [
        pltpu.make_async_copy(gain_hbm, gain_ref, sems.at[1]),
        pltpu.make_async_copy(w_hbm, w_ref, sems.at[2]),
    ]
    for copy in later:
        copy.start()
    count_copy.wait()
    for g, graph in enumerate(graphs):
        h_ref, nrm_ref, sel_ref = graph_outs[g]
        rows_dev = h_ref.shape[0]
        bnd = on_all.shape[1]
        own, half = rows_dev // TILE, bnd // TILE
        for copy in small[g]:
            copy.wait()
        counts = count_ref[...]
        here = lax.broadcasted_iota(jnp.int32, counts.shape, 1) == graph
        live = jnp.sum(jnp.where(here, counts, 0), axis=1, keepdims=True)
        raw = rows_all[g]
        lane = lax.broadcasted_iota(jnp.int32, raw.shape, 1)
        rows = jnp.where(lane < live, raw, -1).astype(F32)
        first = jnp.broadcast_to(rows[0:1, :], (TILE, bnd))
        second = jnp.broadcast_to(rows[1:2, :], (TILE, bnd))
        for at, picked in ((0, jnp.where(even, second, first)), (bnd, jnp.where(even, first, second))):
            column = picked.T
            for c in range(rows_dev // TILE):
                ids = lax.broadcasted_iota(jnp.int32, (bnd, TILE), 1) + c * TILE
                hit = column == ids.astype(F32)
                sel_ref[at : at + bnd, c * TILE : (c + 1) * TILE] = jnp.where(hit, 1.0, 0.0).astype(BF)
        t = src_all[g]
        left = jnp.where(even, own + half, own)
        right = jnp.where(even, own, own + half)
        table = jnp.where(t < half, left + t, jnp.where(t < half + own, t - half, right + t - half - own))
        for i in range(own):
            for k in range(K):
                tables[g][i * K + k : i * K + k + 1, :] = jnp.broadcast_to(table[k : k + 1, i : i + 1], (1, TILE))
        for c, copy in enumerate(feat_copies[g]):
            copy.wait()
            step = rows_dev // len(feat_copies[g])
            block = slice(c * step, (c + 1) * step)
            nrm_ref[block, :] = normalise(h_ref[block, :].astype(F32))
        send_rows(sel_ref, nrm_ref, on_all.at[g], off_all.at[g])
    for copy in later:
        copy.wait()
    scale(w_ref, gain_ref, scaled_ref)
    mine_ref[...] = scaled_ref[dom_parity()]


def fetch_body(per_section, val_ref, after_ref, *refs):
    outs, sems = refs[:per_section], refs[per_section]
    copies = []
    for g, out in enumerate(outs):
        copies += chunked(val_ref.at[graph_of(g, per_section)], out, sems.at[g])
    for copy in copies:
        copy.wait()


def scale(w_ref, gain_ref, out_ref):
    width = w_ref.shape[1]
    gain = gain_ref[...].astype(F32)
    for k in range(w_ref.shape[0]):
        column = jnp.broadcast_to(gain[k : k + 1, :], (width, width)).T
        out_ref[k] = (w_ref[k].astype(F32) * column).astype(BF)


def pack_body(*refs):
    refs = refs[-4:]
    for k, part in enumerate(refs[:-1]):
        refs[-1][k] = part[...]


def order_body(scaled_ref, mine_ref, swapped_ref, out_ref):
    section = lax.axis_index("section")
    parity = dom_parity()
    count = mine_ref.shape[0] + 1
    for k in range(2):
        out_ref[section * 2 + k] = scaled_ref[k]
    for shift in range(1, count):
        source = lax.rem(section - shift + count, count)
        out_ref[source * 2 + parity] = mine_ref[shift - 1]
        out_ref[source * 2 + 1 - parity] = swapped_ref[shift - 1]


def layer_body(layer, graph, last, others, idx_ref, h_ref, nrm_ref, on_in, off_in, tv_ref, sel_ref, w_ref, *rest):
    done, rest = rest[:others], rest[others:]
    if last and others:
        out_ref, ext, agg, out_h, sems = rest
        copies = [pltpu.make_async_copy(done[g], out_ref.at[g], sems.at[g]) for g in range(others)]
        for copy in copies:
            copy.start()
    elif last:
        out_h, ext, agg = rest
    else:
        out_h, out_n, on_ref, off_ref, ext, agg = rest
    if len(on_in.shape) == 3:
        on_in, off_in = on_in.at[graph], off_in.at[graph]
    rows_dev = h_ref.shape[0]
    bnd = on_in.shape[0]
    own, half = rows_dev // TILE, bnd // TILE
    index = [idx_ref[j, 0] for j in range(own * K)]
    ext[0:own] = nrm_ref[...].reshape(own, TILE, -1)
    ext[own : own + half] = on_in[...].reshape(half, TILE, -1)
    ext[own + half : own + 2 * half] = off_in[...].reshape(half, TILE, -1)
    for i in range(own):
        picked = [ext[index[i * K + k]] for k in range(K)]
        agg[i * TILE : (i + 1) * TILE, :] = jnp.dot(
            tv_ref[i * TILE : (i + 1) * TILE, :], jnp.concatenate(picked, axis=0), preferred_element_type=F32
        ).astype(BF)
    step = 256
    for r in range(0, rows_dev, step):
        rows = slice(r, r + step)
        update = jnp.dot(agg[rows, :], w_ref[layer], preferred_element_type=F32)
        new = (h_ref[rows, :].astype(F32) + update).astype(BF)
        out_h[rows, :] = new
        if last and others:
            at = pl.ds(r, step)
            copies.append(pltpu.make_async_copy(out_h.at[at], out_ref.at[others, at], sems.at[others + r // step]))
            copies[-1].start()
        if not last:
            out_n[rows, :] = normalise(new.astype(F32))
    if not last:
        send_rows(sel_ref, out_n, on_ref, off_ref)
    elif others:
        for copy in copies:
            copy.wait()


def on_device(features, tile_src, tile_val, boundary_rows, boundary_count, weights, gains):
    sections = lax.axis_size("section")
    doms = lax.axis_size("dom")
    graphs, rows_dev, width = features.shape
    bnd = boundary_rows.shape[-1]
    per_section = graphs // sections
    layers = weights.shape[0] * sections
    tiles = rows_dev // TILE
    on_pairs = [(i, i ^ 1) for i in range(doms)]
    off_pairs = [(i, (i + (1 if i % 2 else -1)) % doms) for i in range(doms)]

    def exchange(on, off):
        return lax.ppermute(on, "dom", on_pairs), lax.ppermute(off, "dom", off_pairs)

    tile_src = jnp.swapaxes(tile_src, 1, 2)
    boundary_count = jnp.swapaxes(boundary_count, 0, 1)
    features, tile_val, boundary_rows, boundary_count, tile_src, weights, gains = (
        pltpu.with_memory_space_constraint(x, pltpu.HBM)
        for x in (features, tile_val, boundary_rows, boundary_count, tile_src, weights, gains)
    )
    square = (width, width)
    per_graph = [(rows_dev, width), (rows_dev, width), (2 * bnd, rows_dev)]
    results = call(
        functools.partial(prologue_body, per_section),
        per_graph * per_section + [(per_section, bnd, width)] * 2 + [weights.shape, square],
        [HBM] * 6,
        "prologue",
        [
            pltpu.VMEM((per_section, 2, bnd), jnp.int32),
            pltpu.VMEM((2, graphs), jnp.int32),
            pltpu.VMEM((per_section, K, tiles), jnp.int32),
            pltpu.VMEM(weights.shape, BF),
            pltpu.VMEM(gains.shape, BF),
            pltpu.SemaphoreType.DMA((3,)),
            pltpu.SemaphoreType.DMA((per_section, 2)),
            pltpu.SemaphoreType.DMA((per_section, 4)),
        ],
        limit=16,
        ints=[(tiles * K, TILE)] * per_section,
    )(features, boundary_rows, boundary_count, tile_src, weights, gains)
    on_all, off_all, scaled, mine, *tables = results[3 * per_section :]
    on_all = lax.ppermute(on_all, "dom", on_pairs)
    off_all = lax.ppermute(off_all, "dom", off_pairs)
    state = []
    for g in range(per_section):
        h, nrm, sel = results[3 * g : 3 * g + 3]
        state.append([h, nrm, on_all, off_all, sel, tables[g]])
    values = call(
        functools.partial(fetch_body, per_section),
        [(rows_dev, K * TILE)] * per_section,
        [HBM, VMEM],
        "fetch",
        [pltpu.SemaphoreType.DMA((per_section, 4))],
    )(tile_val, on_all)
    parts = [
        lax.ppermute(mine, "section", [(i, (i + shift) % sections) for i in range(sections)])
        for shift in range(1, sections)
    ]
    packed = call(pack_body, [(sections - 1, *square)], [VMEM] * (sections + 1), "pack")(off_all, values[0], *parts)[0]
    swapped = lax.ppermute(packed, "dom", on_pairs)
    w_all = call(order_body, [(layers, *square)], [VMEM] * 3, "order")(scaled, packed, swapped)[0]
    outputs = []
    for layer in range(layers):
        last = layer == layers - 1
        for g in range(per_section):
            h, nrm, on, off, sel, idx = state[g]
            scratch = [pltpu.VMEM((tiles + 2 * bnd // TILE, TILE, width), BF), pltpu.VMEM((rows_dev, width), BF)]
            final = last and g == per_section - 1
            others = len(outputs) if final else 0
            if final:
                outs = [(per_section, rows_dev, width)]
                scratch += [pltpu.VMEM((rows_dev, width), BF), pltpu.SemaphoreType.DMA((others + 4,))]
            elif last:
                outs = [(rows_dev, width)]
            else:
                outs = [(rows_dev, width), (rows_dev, width), (bnd, width), (bnd, width)]
            result = call(
                functools.partial(layer_body, layer, g, last, others),
                outs,
                [VMEM] * (8 + others),
                "layer",
                scratch,
                flops=1_000_000,
                hbm_out=final,
            )(idx, h, nrm, on, off, values[g], sel, w_all, *outputs[:others])
            if last:
                outputs.append(result[0])
            else:
                h, nrm, on, off = result
                state[g] = [h, nrm, *exchange(on, off), sel, idx]
    return outputs[-1]


def solution(mesh):
    in_specs = (
        P(None, "dom", None),
        P(None, "dom", None),
        P(None, "dom", None),
        P(None, "dom", None),
        P(None, "dom"),
        P("section", None, None),
        P("section", None),
    )
    return jax.shard_map(
        on_device, mesh=mesh, in_specs=in_specs, out_specs=P("section", "dom", None), check_vma=False
    )
```

```python
import functools

import jax
import jax.numpy as jnp
from jax import lax
from jax.experimental import pallas as pl
from jax.experimental.pallas import tpu as pltpu
from jax.sharding import PartitionSpec as P

TILE = 128
K = 4
EPS = 1e-06
BF = jnp.bfloat16
F32 = jnp.float32
VMEM = pl.BlockSpec(memory_space=pltpu.VMEM)
HBM = pl.BlockSpec(memory_space=pltpu.HBM)


def call(body, outs, in_specs, name, scratch=(), limit=8, flops=0, ints=(), hbm_out=False):
    return pl.pallas_call(
        body,
        out_shape=[jax.ShapeDtypeStruct(s, BF) for s in outs] + [jax.ShapeDtypeStruct(s, jnp.int32) for s in ints],
        in_specs=in_specs,
        out_specs=[HBM if hbm_out else VMEM] * (len(outs) + len(ints)),
        scratch_shapes=list(scratch),
        name=name,
        cost_estimate=pl.CostEstimate(flops=flops, bytes_accessed=1 << 10, transcendentals=0),
        compiler_params=pltpu.CompilerParams(vmem_limit_bytes=limit << 20),
    )


def normalise(hidden):
    mean = jnp.mean(hidden * hidden, axis=-1, keepdims=True)
    return jnp.maximum(hidden * lax.rsqrt(mean + EPS), 0.0).astype(BF)


def send_rows(chooser_ref, normed_ref, on_ref, off_ref):
    bnd = on_ref.shape[0]
    for at, out in ((bnd, off_ref), (0, on_ref)):
        out[...] = jnp.dot(
            chooser_ref[at : at + bnd, :], normed_ref[...], preferred_element_type=F32
        ).astype(BF)


def dom_parity():
    return lax.rem(lax.axis_index("dom"), 2)


def graph_of(local, per_section):
    return lax.axis_index("section") * per_section + local


def chunked(source, target, sems):
    count = sems.shape[0]
    step = target.shape[0] // count
    copies = []
    for c in range(count):
        rows = pl.ds(c * step, step)
        copies.append(pltpu.make_async_copy(source.at[rows], target.at[rows], sems.at[c]))
    for copy in copies:
        copy.start()
    return copies


def prologue_body(local, per_section, *refs):
    feat, rows_hbm, count_hbm, src_hbm, before_ref = refs[:5]
    h_ref, nrm_ref, sel_ref, on_ref, off_ref, idx_ref = refs[5:11]
    rows_ref, count_ref, src_ref, sems, feat_sems = refs[11:]
    if local:
        for g in range(local):
            on_ref[g] = before_ref[g]
        on_ref = on_ref.at[local]
    else:
        on_ref = on_ref.at[0]
    even = dom_parity() == 0
    graph = graph_of(local, per_section)
    small = [
        pltpu.make_async_copy(rows_hbm.at[graph], rows_ref, sems.at[0]),
        pltpu.make_async_copy(count_hbm, count_ref, sems.at[1]),
        pltpu.make_async_copy(src_hbm.at[graph], src_ref, sems.at[2]),
    ]
    for copy in small:
        copy.start()
    feat_copies = chunked(feat.at[graph], h_ref, feat_sems)
    for copy in small:
        copy.wait()
    rows_dev = h_ref.shape[0]
    bnd = off_ref.shape[0]
    own, half = rows_dev // TILE, bnd // TILE
    counts = count_ref[...]
    here = lax.broadcasted_iota(jnp.int32, counts.shape, 1) == graph
    live = jnp.sum(jnp.where(here, counts, 0), axis=1, keepdims=True)
    raw = rows_ref[...]
    lane = lax.broadcasted_iota(jnp.int32, raw.shape, 1)
    rows = jnp.where(lane < live, raw, -1).astype(F32)
    first = jnp.broadcast_to(rows[0:1, :], (TILE, bnd))
    second = jnp.broadcast_to(rows[1:2, :], (TILE, bnd))
    for at, picked in ((0, jnp.where(even, second, first)), (bnd, jnp.where(even, first, second))):
        column = picked.T
        for c in range(rows_dev // TILE):
            ids = lax.broadcasted_iota(jnp.int32, (bnd, TILE), 1) + c * TILE
            hit = column == ids.astype(F32)
            sel_ref[at : at + bnd, c * TILE : (c + 1) * TILE] = jnp.where(hit, 1.0, 0.0).astype(BF)
    t = src_ref[...]
    left = jnp.where(even, own + half, own)
    right = jnp.where(even, own, own + half)
    table = jnp.where(t < half, left + t, jnp.where(t < half + own, t - half, right + t - half - own))
    for i in range(own):
        for k in range(K):
            idx_ref[i * K + k : i * K + k + 1, :] = jnp.broadcast_to(table[k : k + 1, i : i + 1], (1, TILE))
    for c, copy in enumerate(feat_copies):
        copy.wait()
        step = rows_dev // len(feat_copies)
        block = slice(c * step, (c + 1) * step)
        nrm_ref[block, :] = normalise(h_ref[block, :].astype(F32))
    send_rows(sel_ref, nrm_ref, on_ref, off_ref)


def fetch_body(per_section, val_ref, *refs):
    outs, sems = refs[:per_section], refs[per_section]
    copies = []
    for g, out in enumerate(outs):
        copies += chunked(val_ref.at[graph_of(g, per_section)], out, sems.at[g])
    for copy in copies:
        copy.wait()


def scale_body(w_hbm, gain_hbm, out_ref, mine_ref, w_ref, gain_ref, sems):
    copies = [
        pltpu.make_async_copy(w_hbm, w_ref, sems.at[0]),
        pltpu.make_async_copy(gain_hbm, gain_ref, sems.at[1]),
    ]
    for copy in copies:
        copy.start()
    for copy in copies:
        copy.wait()
    width = w_ref.shape[1]
    gain = gain_ref[...].astype(F32)
    for k in range(w_ref.shape[0]):
        column = jnp.broadcast_to(gain[k : k + 1, :], (width, width)).T
        out_ref[k] = (w_ref[k].astype(F32) * column).astype(BF)
    mine_ref[...] = out_ref[dom_parity()]


def pack_body(*refs):
    refs = refs[-4:]
    for k, part in enumerate(refs[:-1]):
        refs[-1][k] = part[...]


def order_body(scaled_ref, mine_ref, swapped_ref, out_ref):
    section = lax.axis_index("section")
    parity = dom_parity()
    count = mine_ref.shape[0] + 1
    for k in range(2):
        out_ref[section * 2 + k] = scaled_ref[k]
    for shift in range(1, count):
        source = lax.rem(section - shift + count, count)
        out_ref[source * 2 + parity] = mine_ref[shift - 1]
        out_ref[source * 2 + 1 - parity] = swapped_ref[shift - 1]


def layer_body(layer, graph, last, others, idx_ref, h_ref, nrm_ref, on_in, off_in, tv_ref, sel_ref, w_ref, *rest):
    done, rest = rest[:others], rest[others:]
    if last and others:
        out_ref, ext, agg, out_h, sems = rest
        copies = [pltpu.make_async_copy(done[g], out_ref.at[g], sems.at[g]) for g in range(others)]
        for copy in copies:
            copy.start()
    elif last:
        out_h, ext, agg = rest
    else:
        out_h, out_n, on_ref, off_ref, ext, agg = rest
    if len(on_in.shape) == 3:
        on_in = on_in.at[graph]
    rows_dev = h_ref.shape[0]
    bnd = on_in.shape[0]
    own, half = rows_dev // TILE, bnd // TILE
    index = [idx_ref[j, 0] for j in range(own * K)]
    ext[0:own] = nrm_ref[...].reshape(own, TILE, -1)
    ext[own : own + half] = on_in[...].reshape(half, TILE, -1)
    ext[own + half : own + 2 * half] = off_in[...].reshape(half, TILE, -1)
    for i in range(own):
        picked = [ext[index[i * K + k]] for k in range(K)]
        agg[i * TILE : (i + 1) * TILE, :] = jnp.dot(
            tv_ref[i * TILE : (i + 1) * TILE, :], jnp.concatenate(picked, axis=0), preferred_element_type=F32
        ).astype(BF)
    step = 256
    for r in range(0, rows_dev, step):
        rows = slice(r, r + step)
        update = jnp.dot(agg[rows, :], w_ref[layer], preferred_element_type=F32)
        new = (h_ref[rows, :].astype(F32) + update).astype(BF)
        out_h[rows, :] = new
        if last and others:
            at = pl.ds(r, step)
            copies.append(pltpu.make_async_copy(out_h.at[at], out_ref.at[others, at], sems.at[others + r // step]))
            copies[-1].start()
        if not last:
            out_n[rows, :] = normalise(new.astype(F32))
    if not last:
        send_rows(sel_ref, out_n, on_ref, off_ref)
    elif others:
        for copy in copies:
            copy.wait()


def on_device(features, tile_src, tile_val, boundary_rows, boundary_count, weights, gains):
    sections = lax.axis_size("section")
    doms = lax.axis_size("dom")
    graphs, rows_dev, width = features.shape
    bnd = boundary_rows.shape[-1]
    per_section = graphs // sections
    layers = weights.shape[0] * sections
    tiles = rows_dev // TILE
    on_pairs = [(i, i ^ 1) for i in range(doms)]
    off_pairs = [(i, (i + (1 if i % 2 else -1)) % doms) for i in range(doms)]

    def exchange(on, off):
        return lax.ppermute(on, "dom", on_pairs), lax.ppermute(off, "dom", off_pairs)

    tile_src = jnp.swapaxes(tile_src, 1, 2)
    boundary_count = jnp.swapaxes(boundary_count, 0, 1)
    features, tile_val, boundary_rows, boundary_count, tile_src, weights, gains = (
        pltpu.with_memory_space_constraint(x, pltpu.HBM)
        for x in (features, tile_val, boundary_rows, boundary_count, tile_src, weights, gains)
    )
    square = (width, width)
    square = (width, width)
    scaled, mine = call(
        scale_body,
        [weights.shape, square],
        [HBM] * 2,
        "scale",
        [pltpu.VMEM(weights.shape, BF), pltpu.VMEM(gains.shape, BF), pltpu.SemaphoreType.DMA((2,))],
    )(weights, gains)
    on_all = mine
    state = []
    for g in range(per_section):
        h, nrm, sel, on_all, off, idx = call(
            functools.partial(prologue_body, g, per_section),
            [(rows_dev, width), (rows_dev, width), (2 * bnd, rows_dev), (g + 1, bnd, width), (bnd, width)],
            [HBM] * 4 + [VMEM],
            "prologue",
            [
                pltpu.VMEM((2, bnd), jnp.int32),
                pltpu.VMEM((2, graphs), jnp.int32),
                pltpu.VMEM((K, tiles), jnp.int32),
                pltpu.SemaphoreType.DMA((3,)),
                pltpu.SemaphoreType.DMA((4,)),
            ],
            ints=[(tiles * K, TILE)],
        )(features, boundary_rows, boundary_count, tile_src, on_all)
        state.append([h, nrm, None, lax.ppermute(off, "dom", off_pairs), sel, idx])
    on_all = lax.ppermute(on_all, "dom", on_pairs)
    for entry in state:
        entry[2] = on_all
    values = call(
        functools.partial(fetch_body, per_section),
        [(rows_dev, K * TILE)] * per_section,
        [HBM],
        "fetch",
        [pltpu.SemaphoreType.DMA((per_section, 4))],
    )(tile_val)
    parts = [
        lax.ppermute(mine, "section", [(i, (i + shift) % sections) for i in range(sections)])
        for shift in range(1, sections)
    ]
    packed = call(pack_body, [(sections - 1, *square)], [VMEM] * (sections + 1), "pack", flops=3_000_000_000)(values[0], state[-1][1], *parts)[0]
    packed, state[0][3] = lax.optimization_barrier((packed, state[0][3]))
    swapped = lax.ppermute(packed, "dom", on_pairs)
    w_all = call(order_body, [(layers, *square)], [VMEM] * 3, "order")(scaled, packed, swapped)[0]
    outputs = []
    for layer in range(layers):
        last = layer == layers - 1
        for g in range(per_section):
            h, nrm, on, off, sel, idx = state[g]
            scratch = [pltpu.VMEM((tiles + 2 * bnd // TILE, TILE, width), BF), pltpu.VMEM((rows_dev, width), BF)]
            final = last and g == per_section - 1
            others = len(outputs) if final else 0
            if final:
                outs = [(per_section, rows_dev, width)]
                scratch += [pltpu.VMEM((rows_dev, width), BF), pltpu.SemaphoreType.DMA((others + 4,))]
            elif last:
                outs = [(rows_dev, width)]
            else:
                outs = [(rows_dev, width), (rows_dev, width), (bnd, width), (bnd, width)]
            result = call(
                functools.partial(layer_body, layer, g, last, others),
                outs,
                [VMEM] * (8 + others),
                "layer",
                scratch,
                flops=1_000_000,
                hbm_out=final,
            )(idx, h, nrm, on, off, values[g], sel, w_all, *outputs[:others])
            if last:
                outputs.append(result[0])
            else:
                h, nrm, on, off = result
                state[g] = [h, nrm, *exchange(on, off), sel, idx]
    return outputs[-1]


def solution(mesh):
    in_specs = (
        P(None, "dom", None),
        P(None, "dom", None),
        P(None, "dom", None),
        P(None, "dom", None),
        P(None, "dom"),
        P("section", None, None),
        P("section", None),
    )
    return jax.shard_map(
        on_device, mesh=mesh, in_specs=in_specs, out_specs=P("section", "dom", None), check_vma=False
    )
```

```python
import functools

import jax
import jax.numpy as jnp
from jax import lax
from jax.experimental import pallas as pl
from jax.experimental.pallas import tpu as pltpu
from jax.sharding import PartitionSpec as P

TILE = 128
K = 4
EPS = 1e-06
BF = jnp.bfloat16
F32 = jnp.float32
VMEM = pl.BlockSpec(memory_space=pltpu.VMEM)
HBM = pl.BlockSpec(memory_space=pltpu.HBM)


def call(body, outs, in_specs, name, scratch=(), limit=8, flops=0, ints=(), hbm_out=False):
    return pl.pallas_call(
        body,
        out_shape=[jax.ShapeDtypeStruct(s, BF) for s in outs] + [jax.ShapeDtypeStruct(s, jnp.int32) for s in ints],
        in_specs=in_specs,
        out_specs=[HBM if hbm_out else VMEM] * (len(outs) + len(ints)),
        scratch_shapes=list(scratch),
        name=name,
        cost_estimate=pl.CostEstimate(flops=flops, bytes_accessed=1 << 10, transcendentals=0),
        compiler_params=pltpu.CompilerParams(vmem_limit_bytes=limit << 20),
    )


def normalise(hidden):
    mean = jnp.mean(hidden * hidden, axis=-1, keepdims=True)
    return jnp.maximum(hidden * lax.rsqrt(mean + EPS), 0.0).astype(BF)


def send_rows(chooser_ref, normed_ref, on_ref, off_ref):
    bnd = on_ref.shape[0]
    for at, out in ((bnd, off_ref), (0, on_ref)):
        out[...] = jnp.dot(
            chooser_ref[at : at + bnd, :], normed_ref[...], preferred_element_type=F32
        ).astype(BF)


def dom_parity():
    return lax.rem(lax.axis_index("dom"), 2)


def graph_of(local, per_section):
    return lax.axis_index("section") * per_section + local


def chunked(source, target, sems):
    count = sems.shape[0]
    step = target.shape[0] // count
    copies = []
    for c in range(count):
        rows = pl.ds(c * step, step)
        copies.append(pltpu.make_async_copy(source.at[rows], target.at[rows], sems.at[c]))
    for copy in copies:
        copy.start()
    return copies


def prologue_body(local, per_section, *refs):
    if local:
        feat, rows_hbm, count_hbm, src_hbm, before_ref = refs[:5]
        h_ref, nrm_ref, sel_ref, on_ref, off_ref, idx_ref = refs[5:11]
        rows_ref, count_ref, src_ref, sems, feat_sems = refs[11:]
    else:
        h_ref, rows_ref, count_ref, src_ref, _ = refs[:5]
        nrm_ref, sel_ref, on_ref, off_ref, idx_ref = refs[5:10]
    if local:
        for g in range(local):
            on_ref[g] = before_ref[g]
        on_ref = on_ref.at[local]
    else:
        on_ref = on_ref.at[0]
    even = dom_parity() == 0
    graph = graph_of(local, per_section)
    feat_copies = [None] * 4
    if local:
        small = [
            pltpu.make_async_copy(rows_hbm.at[graph], rows_ref, sems.at[0]),
            pltpu.make_async_copy(count_hbm, count_ref, sems.at[1]),
            pltpu.make_async_copy(src_hbm.at[graph], src_ref, sems.at[2]),
        ]
        for copy in small:
            copy.start()
        feat_copies = chunked(feat.at[graph], h_ref, feat_sems)
        for copy in small:
            copy.wait()
    rows_dev = h_ref.shape[0]
    bnd = off_ref.shape[0]
    own, half = rows_dev // TILE, bnd // TILE
    counts = count_ref[...]
    here = lax.broadcasted_iota(jnp.int32, counts.shape, 1) == graph
    live = jnp.sum(jnp.where(here, counts, 0), axis=1, keepdims=True)
    raw = rows_ref[...]
    lane = lax.broadcasted_iota(jnp.int32, raw.shape, 1)
    rows = jnp.where(lane < live, raw, -1).astype(F32)
    first = jnp.broadcast_to(rows[0:1, :], (TILE, bnd))
    second = jnp.broadcast_to(rows[1:2, :], (TILE, bnd))
    for at, picked in ((0, jnp.where(even, second, first)), (bnd, jnp.where(even, first, second))):
        column = picked.T
        for c in range(rows_dev // TILE):
            ids = lax.broadcasted_iota(jnp.int32, (bnd, TILE), 1) + c * TILE
            hit = column == ids.astype(F32)
            sel_ref[at : at + bnd, c * TILE : (c + 1) * TILE] = jnp.where(hit, 1.0, 0.0).astype(BF)
    t = src_ref[...]
    left = jnp.where(even, own + half, own)
    right = jnp.where(even, own, own + half)
    table = jnp.where(t < half, left + t, jnp.where(t < half + own, t - half, right + t - half - own))
    for i in range(own):
        for k in range(K):
            idx_ref[i * K + k : i * K + k + 1, :] = jnp.broadcast_to(table[k : k + 1, i : i + 1], (1, TILE))
    for c, copy in enumerate(feat_copies):
        if local:
            copy.wait()
        step = rows_dev // len(feat_copies)
        block = slice(c * step, (c + 1) * step)
        nrm_ref[block, :] = normalise(h_ref[block, :].astype(F32))
    send_rows(sel_ref, nrm_ref, on_ref, off_ref)


def fetch_body(per_section, val_ref, *refs):
    outs, sems = refs[:per_section], refs[per_section]
    copies = []
    for g, out in enumerate(outs):
        copies += chunked(val_ref.at[graph_of(g, per_section)], out, sems.at[g])
    for copy in copies:
        copy.wait()


def scale_body(per_section, w_hbm, gain_hbm, feat, rows_hbm, count_hbm, src_hbm, *refs):
    out_ref, mine_ref, h_ref, rows_ref, count_ref, src_ref, w_ref, gain_ref, sems, feat_sems = refs
    graph = graph_of(0, per_section)
    copies = [
        pltpu.make_async_copy(w_hbm, w_ref, sems.at[0]),
        pltpu.make_async_copy(gain_hbm, gain_ref, sems.at[1]),
    ]
    others = [
        pltpu.make_async_copy(rows_hbm.at[graph], rows_ref, sems.at[2]),
        pltpu.make_async_copy(count_hbm, count_ref, sems.at[3]),
        pltpu.make_async_copy(src_hbm.at[graph], src_ref, sems.at[4]),
    ]
    for copy in copies + others:
        copy.start()
    others += chunked(feat.at[graph], h_ref, feat_sems)
    for copy in copies:
        copy.wait()
    width = w_ref.shape[1]
    gain = gain_ref[...].astype(F32)
    for k in range(w_ref.shape[0]):
        column = jnp.broadcast_to(gain[k : k + 1, :], (width, width)).T
        out_ref[k] = (w_ref[k].astype(F32) * column).astype(BF)
    mine_ref[...] = out_ref[dom_parity()]
    for copy in others:
        copy.wait()


def pack_body(*refs):
    refs = refs[-4:]
    for k, part in enumerate(refs[:-1]):
        refs[-1][k] = part[...]


def order_body(scaled_ref, mine_ref, swapped_ref, out_ref):
    section = lax.axis_index("section")
    parity = dom_parity()
    count = mine_ref.shape[0] + 1
    for k in range(2):
        out_ref[section * 2 + k] = scaled_ref[k]
    for shift in range(1, count):
        source = lax.rem(section - shift + count, count)
        out_ref[source * 2 + parity] = mine_ref[shift - 1]
        out_ref[source * 2 + 1 - parity] = swapped_ref[shift - 1]


def layer_body(layer, graph, last, others, idx_ref, h_ref, nrm_ref, on_in, off_in, tv_ref, sel_ref, w_ref, *rest):
    done, rest = rest[:others], rest[others:]
    if last and others:
        out_ref, ext, agg, out_h, sems = rest
        copies = [pltpu.make_async_copy(done[g], out_ref.at[g], sems.at[g]) for g in range(others)]
        for copy in copies:
            copy.start()
    elif last:
        out_h, ext, agg = rest
    else:
        out_h, out_n, on_ref, off_ref, ext, agg = rest
    if len(on_in.shape) == 3:
        on_in = on_in.at[graph]
    rows_dev = h_ref.shape[0]
    bnd = on_in.shape[0]
    own, half = rows_dev // TILE, bnd // TILE
    index = [idx_ref[j, 0] for j in range(own * K)]
    ext[0:own] = nrm_ref[...].reshape(own, TILE, -1)
    ext[own : own + half] = on_in[...].reshape(half, TILE, -1)
    ext[own + half : own + 2 * half] = off_in[...].reshape(half, TILE, -1)
    for i in range(own):
        picked = [ext[index[i * K + k]] for k in range(K)]
        agg[i * TILE : (i + 1) * TILE, :] = jnp.dot(
            tv_ref[i * TILE : (i + 1) * TILE, :], jnp.concatenate(picked, axis=0), preferred_element_type=F32
        ).astype(BF)
    step = 256
    for r in range(0, rows_dev, step):
        rows = slice(r, r + step)
        update = jnp.dot(agg[rows, :], w_ref[layer], preferred_element_type=F32)
        new = (h_ref[rows, :].astype(F32) + update).astype(BF)
        out_h[rows, :] = new
        if last and others:
            at = pl.ds(r, step)
            copies.append(pltpu.make_async_copy(out_h.at[at], out_ref.at[others, at], sems.at[others + r // step]))
            copies[-1].start()
        if not last:
            out_n[rows, :] = normalise(new.astype(F32))
    if not last:
        send_rows(sel_ref, out_n, on_ref, off_ref)
    elif others:
        for copy in copies:
            copy.wait()


def on_device(features, tile_src, tile_val, boundary_rows, boundary_count, weights, gains):
    sections = lax.axis_size("section")
    doms = lax.axis_size("dom")
    graphs, rows_dev, width = features.shape
    bnd = boundary_rows.shape[-1]
    per_section = graphs // sections
    layers = weights.shape[0] * sections
    tiles = rows_dev // TILE
    on_pairs = [(i, i ^ 1) for i in range(doms)]
    off_pairs = [(i, (i + (1 if i % 2 else -1)) % doms) for i in range(doms)]

    def exchange(on, off):
        return lax.ppermute(on, "dom", on_pairs), lax.ppermute(off, "dom", off_pairs)

    tile_src = jnp.swapaxes(tile_src, 1, 2)
    boundary_count = jnp.swapaxes(boundary_count, 0, 1)
    features, tile_val, boundary_rows, boundary_count, tile_src, weights, gains = (
        pltpu.with_memory_space_constraint(x, pltpu.HBM)
        for x in (features, tile_val, boundary_rows, boundary_count, tile_src, weights, gains)
    )
    square = (width, width)
    square = (width, width)
    scaled, mine, *given = call(
        functools.partial(scale_body, per_section),
        [weights.shape, square, (rows_dev, width)],
        [HBM] * 6,
        "scale",
        [
            pltpu.VMEM(weights.shape, BF),
            pltpu.VMEM(gains.shape, BF),
            pltpu.SemaphoreType.DMA((5,)),
            pltpu.SemaphoreType.DMA((4,)),
        ],
        ints=[(2, bnd), (2, graphs), (K, tiles)],
    )(weights, gains, features, boundary_rows, boundary_count, tile_src)
    on_all = mine
    state = []
    for g in range(per_section):
        *h, nrm, sel, on_all, off, idx = call(
            functools.partial(prologue_body, g, per_section),
            [(rows_dev, width)] * (2 if g else 1) + [(2 * bnd, rows_dev), (g + 1, bnd, width), (bnd, width)],
            [HBM if g else VMEM] * 4 + [VMEM],
            "prologue",
            [
                pltpu.VMEM((2, bnd), jnp.int32),
                pltpu.VMEM((2, graphs), jnp.int32),
                pltpu.VMEM((K, tiles), jnp.int32),
                pltpu.SemaphoreType.DMA((3,)),
                pltpu.SemaphoreType.DMA((4,)),
            ] if g else [],
            ints=[(tiles * K, TILE)],
        )(*((features, boundary_rows, boundary_count, tile_src) if g else given), on_all)
        h = h[0] if g else given[0]
        state.append([h, nrm, None, lax.ppermute(off, "dom", off_pairs), sel, idx])
    on_all = lax.ppermute(on_all, "dom", on_pairs)
    for entry in state:
        entry[2] = on_all
    values = call(
        functools.partial(fetch_body, per_section),
        [(rows_dev, K * TILE)] * per_section,
        [HBM],
        "fetch",
        [pltpu.SemaphoreType.DMA((per_section, 4))],
    )(tile_val)
    parts = [
        lax.ppermute(mine, "section", [(i, (i + shift) % sections) for i in range(sections)])
        for shift in range(1, sections)
    ]
    packed = call(pack_body, [(sections - 1, *square)], [VMEM] * (sections + 1), "pack", flops=3_000_000_000)(values[0], state[-1][1], *parts)[0]
    packed, state[0][3] = lax.optimization_barrier((packed, state[0][3]))
    swapped = lax.ppermute(packed, "dom", on_pairs)
    w_all = call(order_body, [(layers, *square)], [VMEM] * 3, "order")(scaled, packed, swapped)[0]
    outputs = []
    for layer in range(layers):
        last = layer == layers - 1
        for g in range(per_section):
            h, nrm, on, off, sel, idx = state[g]
            scratch = [pltpu.VMEM((tiles + 2 * bnd // TILE, TILE, width), BF), pltpu.VMEM((rows_dev, width), BF)]
            final = last and g == per_section - 1
            others = len(outputs) if final else 0
            if final:
                outs = [(per_section, rows_dev, width)]
                scratch += [pltpu.VMEM((rows_dev, width), BF), pltpu.SemaphoreType.DMA((others + 4,))]
            elif last:
                outs = [(rows_dev, width)]
            else:
                outs = [(rows_dev, width), (rows_dev, width), (bnd, width), (bnd, width)]
            result = call(
                functools.partial(layer_body, layer, g, last, others),
                outs,
                [VMEM] * (8 + others),
                "layer",
                scratch,
                flops=1_000_000,
                hbm_out=final,
            )(idx, h, nrm, on, off, values[g], sel, w_all, *outputs[:others])
            if last:
                outputs.append(result[0])
            else:
                h, nrm, on, off = result
                state[g] = [h, nrm, *exchange(on, off), sel, idx]
    return outputs[-1]


def solution(mesh):
    in_specs = (
        P(None, "dom", None),
        P(None, "dom", None),
        P(None, "dom", None),
        P(None, "dom", None),
        P(None, "dom"),
        P("section", None, None),
        P("section", None),
    )
    return jax.shard_map(
        on_device, mesh=mesh, in_specs=in_specs, out_specs=P("section", "dom", None), check_vma=False
    )
```

```python
import functools

import jax
import jax.numpy as jnp
from jax import lax
from jax.experimental import pallas as pl
from jax.experimental.pallas import tpu as pltpu
from jax.sharding import PartitionSpec as P

TILE = 128
K = 4
EPS = 1e-06
BF = jnp.bfloat16
F32 = jnp.float32
VMEM = pl.BlockSpec(memory_space=pltpu.VMEM)
HBM = pl.BlockSpec(memory_space=pltpu.HBM)


def call(body, outs, in_specs, name, scratch=(), limit=8, flops=0, ints=(), hbm_out=False):
    return pl.pallas_call(
        body,
        out_shape=[jax.ShapeDtypeStruct(s, BF) for s in outs] + [jax.ShapeDtypeStruct(s, jnp.int32) for s in ints],
        in_specs=in_specs,
        out_specs=[HBM if hbm_out else VMEM] * (len(outs) + len(ints)),
        scratch_shapes=list(scratch),
        name=name,
        cost_estimate=pl.CostEstimate(flops=flops, bytes_accessed=1 << 10, transcendentals=0),
        compiler_params=pltpu.CompilerParams(vmem_limit_bytes=limit << 20),
    )


def normalise(hidden):
    mean = jnp.mean(hidden * hidden, axis=-1, keepdims=True)
    return jnp.maximum(hidden * lax.rsqrt(mean + EPS), 0.0).astype(BF)


def send_rows(chooser_ref, normed_ref, on_ref, off_ref):
    bnd = on_ref.shape[0]
    for at, out in ((bnd, off_ref), (0, on_ref)):
        out[...] = jnp.dot(
            chooser_ref[at : at + bnd, :], normed_ref[...], preferred_element_type=F32
        ).astype(BF)


def dom_parity():
    return lax.rem(lax.axis_index("dom"), 2)


def graph_of(local, per_section):
    return lax.axis_index("section") * per_section + local


def chunked(source, target, sems):
    count = sems.shape[0]
    step = target.shape[0] // count
    copies = []
    for c in range(count):
        rows = pl.ds(c * step, step)
        copies.append(pltpu.make_async_copy(source.at[rows], target.at[rows], sems.at[c]))
    for copy in copies:
        copy.start()
    return copies


def prologue_body(local, per_section, *refs):
    if local:
        feat, rows_hbm, count_hbm, src_hbm, before_ref = refs[:5]
        h_ref, nrm_ref, sel_ref, on_ref, off_ref, idx_ref = refs[5:11]
        rows_ref, count_ref, src_ref, sems, feat_sems = refs[11:]
    else:
        h_ref, rows_ref, count_ref, src_ref, _ = refs[:5]
        nrm_ref, sel_ref, on_ref, off_ref, idx_ref = refs[5:10]
    if local:
        for g in range(local):
            on_ref[g] = before_ref[g]
        on_ref = on_ref.at[local]
    else:
        on_ref = on_ref.at[0]
    even = dom_parity() == 0
    graph = graph_of(local, per_section)
    feat_copies = [None] * 4
    if local:
        small = [
            pltpu.make_async_copy(rows_hbm.at[graph], rows_ref, sems.at[0]),
            pltpu.make_async_copy(count_hbm, count_ref, sems.at[1]),
            pltpu.make_async_copy(src_hbm.at[graph], src_ref, sems.at[2]),
        ]
        for copy in small:
            copy.start()
        feat_copies = chunked(feat.at[graph], h_ref, feat_sems)
        for copy in small:
            copy.wait()
    rows_dev = h_ref.shape[0]
    bnd = off_ref.shape[0]
    own, half = rows_dev // TILE, bnd // TILE
    counts = count_ref[...]
    here = lax.broadcasted_iota(jnp.int32, counts.shape, 1) == graph
    live = jnp.sum(jnp.where(here, counts, 0), axis=1, keepdims=True)
    raw = rows_ref[...]
    lane = lax.broadcasted_iota(jnp.int32, raw.shape, 1)
    rows = jnp.where(lane < live, raw, -1).astype(F32)
    first = jnp.broadcast_to(rows[0:1, :], (TILE, bnd))
    second = jnp.broadcast_to(rows[1:2, :], (TILE, bnd))
    for at, picked in ((0, jnp.where(even, second, first)), (bnd, jnp.where(even, first, second))):
        column = picked.T
        for c in range(rows_dev // TILE):
            ids = lax.broadcasted_iota(jnp.int32, (bnd, TILE), 1) + c * TILE
            hit = column == ids.astype(F32)
            sel_ref[at : at + bnd, c * TILE : (c + 1) * TILE] = jnp.where(hit, 1.0, 0.0).astype(BF)
    t = src_ref[...]
    left = jnp.where(even, own + half, own)
    right = jnp.where(even, own, own + half)
    table = jnp.where(t < half, left + t, jnp.where(t < half + own, t - half, right + t - half - own))
    for i in range(own):
        for k in range(K):
            idx_ref[i * K + k : i * K + k + 1, :] = jnp.broadcast_to(table[k : k + 1, i : i + 1], (1, TILE))
    for c, copy in enumerate(feat_copies):
        if local:
            copy.wait()
        step = rows_dev // len(feat_copies)
        block = slice(c * step, (c + 1) * step)
        nrm_ref[block, :] = normalise(h_ref[block, :].astype(F32))
    send_rows(sel_ref, nrm_ref, on_ref, off_ref)


def fetch_body(per_section, val_ref, *refs):
    outs, sems = refs[:per_section], refs[per_section]
    copies = []
    for g, out in enumerate(outs):
        copies += chunked(val_ref.at[graph_of(g, per_section)], out, sems.at[g])
    for copy in copies:
        copy.wait()


def scale_body(per_section, w_hbm, gain_hbm, feat, rows_hbm, count_hbm, src_hbm, *refs):
    out_ref, mine_ref, h_ref, rows_ref, count_ref, src_ref, w_ref, gain_ref, sems, feat_sems = refs
    graph = graph_of(0, per_section)
    copies = [
        pltpu.make_async_copy(w_hbm, w_ref, sems.at[0]),
        pltpu.make_async_copy(gain_hbm, gain_ref, sems.at[1]),
    ]
    others = [
        pltpu.make_async_copy(rows_hbm.at[graph], rows_ref, sems.at[2]),
        pltpu.make_async_copy(count_hbm, count_ref, sems.at[3]),
        pltpu.make_async_copy(src_hbm.at[graph], src_ref, sems.at[4]),
    ]
    for copy in copies + others:
        copy.start()
    others += chunked(feat.at[graph], h_ref, feat_sems)
    for copy in copies:
        copy.wait()
    width = w_ref.shape[1]
    gain = gain_ref[...].astype(F32)
    for k in range(w_ref.shape[0]):
        column = jnp.broadcast_to(gain[k : k + 1, :], (width, width)).T
        out_ref[k] = (w_ref[k].astype(F32) * column).astype(BF)
    mine_ref[...] = out_ref[dom_parity()]
    for copy in others:
        copy.wait()


def gate_body(after_ref, out_ref):
    out_ref[...] = jnp.zeros_like(out_ref)


def pack_body(*refs):
    refs = refs[-4:]
    for k, part in enumerate(refs[:-1]):
        refs[-1][k] = part[...]


def order_body(scaled_ref, mine_ref, swapped_ref, out_ref):
    section = lax.axis_index("section")
    parity = dom_parity()
    count = mine_ref.shape[0] + 1
    for k in range(2):
        out_ref[section * 2 + k] = scaled_ref[k]
    for shift in range(1, count):
        source = lax.rem(section - shift + count, count)
        out_ref[source * 2 + parity] = mine_ref[shift - 1]
        out_ref[source * 2 + 1 - parity] = swapped_ref[shift - 1]


def layer_body(layer, graph, last, gated, others, idx_ref, h_ref, nrm_ref, on_in, off_in, tv_ref, sel_ref, w_ref, *rest):
    rest = rest[gated:]
    done, rest = rest[:others], rest[others:]
    if last and others:
        out_ref, ext, agg, out_h, sems = rest
        copies = [pltpu.make_async_copy(done[g], out_ref.at[g], sems.at[g]) for g in range(others)]
        for copy in copies:
            copy.start()
    elif last:
        out_h, ext, agg = rest
    else:
        out_h, out_n, on_ref, off_ref, ext, agg = rest
    if len(on_in.shape) == 3:
        on_in = on_in.at[graph]
    rows_dev = h_ref.shape[0]
    bnd = on_in.shape[0]
    own, half = rows_dev // TILE, bnd // TILE
    index = [idx_ref[j, 0] for j in range(own * K)]
    ext[0:own] = nrm_ref[...].reshape(own, TILE, -1)
    ext[own : own + half] = on_in[...].reshape(half, TILE, -1)
    ext[own + half : own + 2 * half] = off_in[...].reshape(half, TILE, -1)
    for i in range(own):
        picked = [ext[index[i * K + k]] for k in range(K)]
        agg[i * TILE : (i + 1) * TILE, :] = jnp.dot(
            tv_ref[i * TILE : (i + 1) * TILE, :], jnp.concatenate(picked, axis=0), preferred_element_type=F32
        ).astype(BF)
    step = 256
    for r in range(0, rows_dev, step):
        rows = slice(r, r + step)
        update = jnp.dot(agg[rows, :], w_ref[layer], preferred_element_type=F32)
        new = (h_ref[rows, :].astype(F32) + update).astype(BF)
        out_h[rows, :] = new
        if last and others:
            at = pl.ds(r, step)
            copies.append(pltpu.make_async_copy(out_h.at[at], out_ref.at[others, at], sems.at[others + r // step]))
            copies[-1].start()
        if not last:
            out_n[rows, :] = normalise(new.astype(F32))
    if not last:
        send_rows(sel_ref, out_n, on_ref, off_ref)
    elif others:
        for copy in copies:
            copy.wait()


def on_device(features, tile_src, tile_val, boundary_rows, boundary_count, weights, gains):
    sections = lax.axis_size("section")
    doms = lax.axis_size("dom")
    graphs, rows_dev, width = features.shape
    bnd = boundary_rows.shape[-1]
    per_section = graphs // sections
    layers = weights.shape[0] * sections
    tiles = rows_dev // TILE
    on_pairs = [(i, i ^ 1) for i in range(doms)]
    off_pairs = [(i, (i + (1 if i % 2 else -1)) % doms) for i in range(doms)]

    def exchange(on, off):
        return lax.ppermute(on, "dom", on_pairs), lax.ppermute(off, "dom", off_pairs)

    tile_src = jnp.swapaxes(tile_src, 1, 2)
    boundary_count = jnp.swapaxes(boundary_count, 0, 1)
    features, tile_val, boundary_rows, boundary_count, tile_src, weights, gains = (
        pltpu.with_memory_space_constraint(x, pltpu.HBM)
        for x in (features, tile_val, boundary_rows, boundary_count, tile_src, weights, gains)
    )
    square = (width, width)
    square = (width, width)
    scaled, mine, *given = call(
        functools.partial(scale_body, per_section),
        [weights.shape, square, (rows_dev, width)],
        [HBM] * 6,
        "scale",
        [
            pltpu.VMEM(weights.shape, BF),
            pltpu.VMEM(gains.shape, BF),
            pltpu.SemaphoreType.DMA((5,)),
            pltpu.SemaphoreType.DMA((4,)),
        ],
        ints=[(2, bnd), (2, graphs), (K, tiles)],
    )(weights, gains, features, boundary_rows, boundary_count, tile_src)
    on_all = mine
    state = []
    for g in range(per_section):
        *h, nrm, sel, on_all, off, idx = call(
            functools.partial(prologue_body, g, per_section),
            [(rows_dev, width)] * (2 if g else 1) + [(2 * bnd, rows_dev), (g + 1, bnd, width), (bnd, width)],
            [HBM if g else VMEM] * 4 + [VMEM],
            "prologue",
            [
                pltpu.VMEM((2, bnd), jnp.int32),
                pltpu.VMEM((2, graphs), jnp.int32),
                pltpu.VMEM((K, tiles), jnp.int32),
                pltpu.SemaphoreType.DMA((3,)),
                pltpu.SemaphoreType.DMA((4,)),
            ] if g else [],
            ints=[(tiles * K, TILE)],
        )(*((features, boundary_rows, boundary_count, tile_src) if g else given), on_all)
        h = h[0] if g else given[0]
        state.append([h, nrm, None, lax.ppermute(off, "dom", off_pairs), sel, idx])
    on_all = lax.ppermute(on_all, "dom", on_pairs)
    for entry in state:
        entry[2] = on_all
    values = call(
        functools.partial(fetch_body, per_section),
        [(rows_dev, K * TILE)] * per_section,
        [HBM],
        "fetch",
        [pltpu.SemaphoreType.DMA((per_section, 4))],
    )(tile_val)
    parts = [
        lax.ppermute(mine, "section", [(i, (i + shift) % sections) for i in range(sections)])
        for shift in range(1, sections)
    ]
    packed = call(pack_body, [(sections - 1, *square)], [VMEM] * (sections + 1), "pack", flops=3_000_000_000)(values[0], state[-1][1], *parts)[0]
    packed, state[0][3] = lax.optimization_barrier((packed, state[0][3]))
    swapped = lax.ppermute(packed, "dom", on_pairs)
    w_all = call(order_body, [(layers, *square)], [VMEM] * 3, "order")(scaled, packed, swapped)[0]
    outputs = []
    for layer in range(layers):
        last = layer == layers - 1
        for g in range(per_section):
            h, nrm, on, off, sel, idx = state[g]
            scratch = [pltpu.VMEM((tiles + 2 * bnd // TILE, TILE, width), BF), pltpu.VMEM((rows_dev, width), BF)]
            final = last and g == per_section - 1
            others = len(outputs) if final else 0
            if final:
                outs = [(per_section, rows_dev, width)]
                scratch += [pltpu.VMEM((rows_dev, width), BF), pltpu.SemaphoreType.DMA((others + 4,))]
            elif last:
                outs = [(rows_dev, width)]
            else:
                outs = [(rows_dev, width), (rows_dev, width), (bnd, width), (bnd, width)]
            gate = [call(gate_body, [(16, TILE)], [VMEM], "gate")(off)[0]] if layer else []
            result = call(
                functools.partial(layer_body, layer, g, last, len(gate), others),
                outs,
                [VMEM] * (8 + len(gate) + others),
                "layer",
                scratch,
                flops=1_000_000,
                hbm_out=final,
            )(idx, h, nrm, on, off, values[g], sel, w_all, *gate, *outputs[:others])
            if last:
                outputs.append(result[0])
            else:
                h, nrm, on, off = result
                state[g] = [h, nrm, *exchange(on, off), sel, idx]
    return outputs[-1]


def solution(mesh):
    in_specs = (
        P(None, "dom", None),
        P(None, "dom", None),
        P(None, "dom", None),
        P(None, "dom", None),
        P(None, "dom"),
        P("section", None, None),
        P("section", None),
    )
    return jax.shard_map(
        on_device, mesh=mesh, in_specs=in_specs, out_specs=P("section", "dom", None), check_vma=False
    )
```
